128 devices in a mesh: pts: 64 (over z, y_hi, x, core), rep: 2 (over y_lo).
Axes of the slice: x: 4, y: 4 (y_hi: 2, y_lo: 2; y = y_hi * 2 + y_lo), z: 4, core: 2. Of those that a mesh axis runs over, the one named last changes fastest.
Arguments:
- points: bfloat16 [262144, 512], P(('rep', 'pts')), parts along dimension 0, may hold values from -6 to 6
- point_row_index: int32 [262144], P(('rep', 'pts')), parts along dimension 0, may hold values from 0 to 131071, as said below
- neighbour_ball_list: int32 [1024, 4], P(('rep', 'pts')), parts along dimension 0, may hold values from 0 to 511, as said below
- attention_norm_gain: float32 [512], replicated, may hold values from 0.1 to 1.9
- query_weight: bfloat16 [512, 512], replicated, may hold values from -0.25 to 0.25
- key_weight: bfloat16 [512, 512], replicated, may hold values from -0.25 to 0.25
- value_weight: bfloat16 [512, 512], replicated, may hold values from -0.25 to 0.25
- pooled_key_weight: bfloat16 [512, 512], replicated, may hold values from -0.75 to 0.75
- pooled_value_weight: bfloat16 [512, 512], replicated, may hold values from -0.75 to 0.75
- head_score_scale: float32 [16], replicated, may hold values from 4 to 16
- output_weight: bfloat16 [512, 512], replicated, may hold values from -0.25 to 0.25
- feedforward_norm_gain: float32 [512], replicated, may hold values from 0.1 to 1.9
- gate_weight: bfloat16 [512, 1024], replicated, may hold values from -0.25 to 0.25
- up_weight: bfloat16 [512, 1024], replicated, may hold values from -0.25 to 0.25
- down_weight: bfloat16 [1024, 512], replicated, may hold values from -0.1875 to 0.1875
Outputs:
- layer_out: bfloat16 [262144, 512], P(('rep', 'pts')), parts along dimension 0
The draws below stay inside these ranges and needn't reach their ends.
There are 2 independent parts, one for each index of `rep`. The reference program is written for one: setup_inputs(seed, part) draws one part's arguments, and reference() takes and returns one part's arrays. A program takes and returns all parts, laid end to end along the dimension named above; an argument that names none is the same for every part. Nothing has to cross between parts.
Inputs may be any that keep to these rules, and one draw needn't show every extreme that they name: point_row_index holds every number of 0 to 131071 once; of the 2048 points of one device (rows d * 2048 to (d + 1) * 2048 - 1 of points) exactly 32 go to the rows of each device. `neighbour_ball_list`: row b starts with b itself; its other three entries are balls on three different devices among those 1 to 4 places away from ball b's device around the loop of devices, ball c lying on device c // 8.
All inputs are finite; a program needn't handle non-finite values.
Results may differ from the reference program's by a relative error of at most 0.012.
Values may be sent and summed in bfloat16 or wider, within the bound.
A program may use at most 128 MiB of HBM per device.

```python
import math
import jax
import jax.numpy as jnp
from jax import lax

D = 512
HEAD_TOTAL = 16
HD = 32
FF = 1024
BALL = 256
POOL = 8
OWNERS = 4
REACH = 4
P_DEV = 2048
POINTS = 131072
NBALLS = 512
CK = 32
SEND = 32


def draw_point_row_index(key, part):
    devices = POINTS // P_DEV
    base_key = jax.random.fold_in(key, 11)
    shuffle_key = jax.random.fold_in(key, 13)

    def dest_inverse(dest_index):
        shuffled = jax.random.permutation(jax.random.fold_in(base_key, dest_index), P_DEV)
        return jnp.argsort(shuffled).astype(jnp.int32)
    inverse = jax.vmap(dest_inverse)(jnp.arange(devices, dtype=jnp.int32))
    table = inverse.reshape(devices, devices, SEND) + (jnp.arange(devices, dtype=jnp.int32) * P_DEV)[:, None, None]
    table = jnp.transpose(table, (1, 0, 2)).reshape(devices, P_DEV)

    def source_order(source_index):
        return jax.random.permutation(jax.random.fold_in(shuffle_key, source_index), P_DEV).astype(jnp.int32)
    orders = jax.vmap(source_order)(jnp.arange(devices, dtype=jnp.int32))
    placed = jnp.take_along_axis(table, orders, axis=1)
    return placed.reshape(POINTS).astype(jnp.int32)


def draw_neighbour_ball_list(key, part):
    devices = POINTS // P_DEV
    per_device = P_DEV // BALL
    base_key = jax.random.fold_in(key, 23)
    steps_up = jnp.arange(1, REACH + 1, dtype=jnp.int32)
    choices_table = jnp.concatenate([-steps_up, steps_up]).astype(jnp.int32)

    def one_ball(ball_index):
        ball_key = jax.random.fold_in(base_key, ball_index)
        shifted = jax.random.permutation(jax.random.fold_in(ball_key, 1), choices_table)[:3]
        blocks = jax.random.randint(jax.random.fold_in(ball_key, 2), (3,), 0, per_device, dtype=jnp.int32)
        home = ball_index // per_device
        others = jnp.mod(home + shifted, devices) * per_device + blocks
        return jnp.concatenate([ball_index[None], others]).astype(jnp.int32)
    return jax.vmap(one_ball)(jnp.arange(NBALLS, dtype=jnp.int32))


def block_levels(key, dims, cuts, least, largest):
    loudness = 1.0
    for axis_at, shards_of in cuts:
        heights = jax.random.uniform(jax.random.fold_in(jax.random.fold_in(key, 6), axis_at), (shards_of,), jnp.float32, least / len(cuts), largest / len(cuts))
        loudness = loudness * jnp.repeat(jnp.exp(heights), dims[axis_at] // shards_of).reshape((-1,) + (1,) * (len(dims) - 1 - axis_at))
    return loudness


def scatter_about(stream_key, dims, scale, bound, cuts=(), held_as=jnp.bfloat16):
    result = jax.random.normal(stream_key, dims, jnp.float32) * scale
    if len(cuts) > 0:
        result = block_levels(stream_key, dims, cuts, -0.22, 0.18) * result
    return jnp.clip(result, min=-bound, max=bound).astype(held_as)


def setup_inputs(seed: int = 0, part: int = 0) -> dict:
    streams_of = jax.random.split(jax.random.key(seed), 16)
    own_keys = jax.random.split(jax.random.fold_in(streams_of[15], part), 16)
    return {
        "points": scatter_about(own_keys[0], (POINTS, D), 1.0, 6.0, ((0, 64),)),
        "point_row_index": draw_point_row_index(jax.random.fold_in(jax.random.fold_in(streams_of[15], part), 71), part),
        "neighbour_ball_list": draw_neighbour_ball_list(jax.random.fold_in(jax.random.fold_in(streams_of[15], part), 71), part),
        "attention_norm_gain": jnp.clip(1.0 + 0.18 * jax.random.normal(streams_of[3], (D,), jnp.float32), 0.1, 1.9),
        "query_weight": scatter_about(streams_of[4], (D, D), D ** -0.5, 0.25),
        "key_weight": scatter_about(streams_of[5], (D, D), D ** -0.5, 0.25),
        "value_weight": scatter_about(streams_of[6], (D, D), D ** -0.5, 0.25),
        "pooled_key_weight": scatter_about(streams_of[7], (D, D), (D // POOL) ** -0.5, 0.75),
        "pooled_value_weight": scatter_about(streams_of[8], (D, D), (D // POOL) ** -0.5, 0.75),
        "head_score_scale": jnp.clip(jnp.exp(jax.random.uniform(streams_of[9], (HEAD_TOTAL,), jnp.float32, math.log(4.0), math.log(16.0))), 4.0, 16.0),
        "output_weight": scatter_about(streams_of[10], (D, D), D ** -0.5, 0.25),
        "feedforward_norm_gain": jnp.clip(1.0 + 0.18 * jax.random.normal(streams_of[11], (D,), jnp.float32), 0.1, 1.9),
        "gate_weight": scatter_about(streams_of[12], (D, FF), D ** -0.5, 0.25),
        "up_weight": scatter_about(streams_of[13], (D, FF), D ** -0.5, 0.25),
        "down_weight": scatter_about(streams_of[14], (FF, D), FF ** -0.5, 0.1875),
    }


def row_norm(values, scale_gain):
    mean_square = lax.optimization_barrier(jnp.mean(values * values, axis=-1, keepdims=True))
    return values * lax.rsqrt(mean_square + 1e-05) * scale_gain

def head_norm(values, head_total):
    shaped = values.reshape(values.shape[0], head_total, -1)
    mean_square = lax.optimization_barrier(jnp.mean(shaped * shaped, axis=-1, keepdims=True))
    return shaped * lax.rsqrt(mean_square + 1e-06)

def ball_attention_layer(query_rows, local_key_rows, local_value_rows, coarse_key_rows, coarse_value_rows, head_score_scale):
    keys_all = jnp.concatenate([local_key_rows, coarse_key_rows], axis=0).astype(jnp.float32)
    values_all = jnp.concatenate([local_value_rows, coarse_value_rows], axis=0).astype(jnp.float32)
    score_matrix = jnp.einsum('qhd,khd->hqk', query_rows.astype(jnp.float32), keys_all)
    score_matrix = score_matrix * (head_score_scale / query_rows.shape[-1])[:, None, None]
    exponent = jnp.exp(score_matrix)
    denominator = lax.optimization_barrier(jnp.sum(exponent, axis=-1, keepdims=True))
    probabilities = (exponent / denominator).astype(jnp.bfloat16)
    attended_rows = jnp.einsum('hqk,khd->qhd', probabilities.astype(jnp.float32), values_all)
    return attended_rows.reshape(query_rows.shape[0], -1).astype(jnp.bfloat16)

def reference(points, point_row_index, neighbour_ball_list, attention_norm_gain, query_weight, key_weight, value_weight, pooled_key_weight, pooled_value_weight, head_score_scale, output_weight, feedforward_norm_gain, gate_weight, up_weight, down_weight):
    head_total = head_score_scale.shape[0]
    grouped = jnp.zeros_like(points).at[point_row_index].set(points)
    normed = row_norm(grouped.astype(jnp.float32), attention_norm_gain).astype(jnp.bfloat16)
    query_rows = head_norm(jnp.dot(normed, query_weight, preferred_element_type=jnp.float32), head_total).astype(jnp.bfloat16)
    local_key_rows = head_norm(jnp.dot(normed, key_weight, preferred_element_type=jnp.float32), head_total).astype(jnp.bfloat16)
    local_value_rows = jnp.dot(normed, value_weight, preferred_element_type=jnp.float32).astype(jnp.bfloat16).reshape(POINTS, head_total, HD)
    pooled = lax.optimization_barrier(jnp.mean(normed.astype(jnp.float32).reshape(POINTS // POOL, POOL, D), axis=1)).astype(jnp.bfloat16)
    comp_key = head_norm(jnp.dot(pooled, pooled_key_weight, preferred_element_type=jnp.float32), head_total).astype(jnp.bfloat16)
    comp_key = comp_key.reshape(NBALLS, CK, head_total, HD)
    comp_value = jnp.dot(pooled, pooled_value_weight, preferred_element_type=jnp.float32).astype(jnp.bfloat16)
    comp_value = comp_value.reshape(NBALLS, CK, head_total, HD)

    def one_ball(ball_index):
        start = (ball_index * BALL).astype(jnp.int32)
        ball_query_rows = lax.dynamic_slice_in_dim(query_rows, start, BALL, 0)
        ball_key_rows = lax.dynamic_slice_in_dim(local_key_rows, start, BALL, 0)
        ball_value_rows = lax.dynamic_slice_in_dim(local_value_rows, start, BALL, 0)
        chosen = neighbour_ball_list[ball_index].astype(jnp.int32)
        coarse_key_rows = jnp.take(comp_key, chosen, axis=0).reshape(OWNERS * CK, head_total, HD)
        coarse_value_rows = jnp.take(comp_value, chosen, axis=0).reshape(OWNERS * CK, head_total, HD)
        return ball_attention_layer(ball_query_rows, ball_key_rows, ball_value_rows, coarse_key_rows, coarse_value_rows, head_score_scale)
    attended_rows = lax.map(one_ball, jnp.arange(NBALLS, dtype=jnp.int32)).reshape(POINTS, D)
    residual = (grouped.astype(jnp.float32) + jnp.dot(attended_rows, output_weight, preferred_element_type=jnp.float32)).astype(jnp.bfloat16)
    ffn_normed = row_norm(residual.astype(jnp.float32), feedforward_norm_gain).astype(jnp.bfloat16)
    gate_proj = jnp.dot(ffn_normed, gate_weight, preferred_element_type=jnp.float32)
    up_proj = jnp.dot(ffn_normed, up_weight, preferred_element_type=jnp.float32)
    hidden = (jax.nn.silu(gate_proj) * up_proj).astype(jnp.bfloat16)
    ball_out = (residual.astype(jnp.float32) + jnp.dot(hidden, down_weight, preferred_element_type=jnp.float32)).astype(jnp.bfloat16)
    return jnp.take(ball_out, point_row_index.astype(jnp.int32), axis=0)
```

```python
import functools
import math

import jax
import jax.numpy as jnp
from jax import lax
from jax.experimental import pallas as pl
from jax.experimental.pallas import tpu as pltpu
from jax.sharding import PartitionSpec as P

BALL = 256
POOL = 8
OWNERS = 4
REACH = 4
D = 512
HEADS = 16
HD = 32
FF = 1024
ROWS = 2048
PEERS = 64
EACH = 32
CK = BALL // POOL
KEYS = BALL + OWNERS * CK
GROUP = 8
NB = ROWS // BALL
MESH = pl.DeviceIdType.MESH
F32 = jnp.float32
BF16 = jnp.bfloat16
VMEM_LIMIT = 56 * 1024 * 1024


def vmem(n):
    return [pl.BlockSpec(memory_space=pltpu.VMEM)] * n


def fixed(shape):
    return pl.BlockSpec(shape, lambda *_: (0,) * len(shape), pipeline_mode=pl.Buffered(1))


def mm(a, b):
    return jnp.dot(a, b, preferred_element_type=F32)


def mm_nt(a, b):
    return lax.dot_general(a, b, (((1,), (1,)), ((), ())), preferred_element_type=F32)


def one_hot_rows(start, count, row):
    ids = lax.broadcasted_iota(jnp.int32, (count, ROWS), 0) + start
    return jnp.where(ids == row, 1.0, 0.0).astype(BF16)


def one_hot_cols(col, count):
    ids = lax.broadcasted_iota(jnp.int32, (count, ROWS), 1)
    return jnp.where(ids == col, 1.0, 0.0).astype(BF16)


def pack_kernel(col_ref, row_ref, x_ref, out_ref, ids_ref, pos_ref):
    step = pl.program_id(0)

    @pl.when(step == 0)
    def _():
        def count(j, acc):
            col = col_ref[pl.ds(pl.multiple_of(j * 256, 256), 256), :]
            less = jnp.where(col < row_ref[...], 1.0, 0.0)
            return acc + jnp.sum(less.reshape(32, 8, ROWS), axis=0)

        acc = lax.fori_loop(0, NB, count, jnp.zeros((8, ROWS), F32))
        pos_ref[...] = jnp.sum(acc, axis=0, keepdims=True).astype(jnp.int32)

    hot = one_hot_rows(step * 256, 256, pos_ref[...])
    out_ref[...] = mm(hot, x_ref[...]).astype(BF16)
    number = row_ref[...]
    high = (number // 2048).astype(F32)
    mid = ((number // 64) % 32).astype(F32)
    low = (number % 64).astype(F32)
    pad = jnp.zeros((5, ROWS), F32)
    parts = jnp.concatenate([high, mid, low, pad], axis=0).astype(BF16)
    back = mm_nt(parts, hot)
    whole = back[0:1] * 2048.0 + back[1:2] * 64.0 + back[2:3]
    whole = whole.astype(jnp.int32)
    ids_ref[0] = whole[:, :128]
    ids_ref[1] = whole[:, 128:]


def pack(col, row, x):
    return pl.pallas_call(
        pack_kernel,
        grid=(NB,),
        in_specs=[fixed((ROWS, 1)), fixed((1, ROWS)), fixed((ROWS, D))],
        out_specs=[
            pl.BlockSpec((256, D), lambda i: (i, 0)),
            pl.BlockSpec((2, 1, 128), lambda i: (i, 0, 0)),
            pl.BlockSpec((1, ROWS), lambda i: (0, 0)),
        ],
        out_shape=[
            jax.ShapeDtypeStruct((ROWS, D), BF16),
            jax.ShapeDtypeStruct((16, 1, 128), jnp.int32),
            jax.ShapeDtypeStruct((1, ROWS), jnp.int32),
        ],
        compiler_params=pltpu.CompilerParams(vmem_limit_bytes=VMEM_LIMIT),
        name="pack",
    )(col, row, x)


def peer(k):
    return lax.rem(lax.axis_index("pts") + k, PEERS)


def greet():
    barrier = pltpu.get_barrier_semaphore()

    def signal(k, carry):
        pl.semaphore_signal(barrier, inc=1, device_id={"pts": peer(k)}, device_id_type=MESH)
        return carry

    lax.fori_loop(1, PEERS, signal, 0)
    pl.semaphore_wait(barrier, PEERS - 1)


def exchange_kernel(with_ids, *refs):
    if with_ids:
        x_ref, i_ref, o_ref, oi_ref, send, recv, isend, irecv, here = refs
    else:
        x_ref, o_ref, send, recv, here = refs
    me = lax.axis_index("pts")
    greet()

    def rows(k):
        d = peer(k)
        return pltpu.make_async_remote_copy(
            src_ref=x_ref.at[d], dst_ref=o_ref.at[me], send_sem=send.at[k],
            recv_sem=recv.at[k], device_id={"pts": d}, device_id_type=MESH)

    def numbers(k):
        d = peer(k)
        return pltpu.make_async_remote_copy(
            src_ref=i_ref.at[d // 4], dst_ref=oi_ref.at[me], send_sem=isend.at[k],
            recv_sem=irecv.at[k], device_id={"pts": d}, device_id_type=MESH)

    def order(k):
        return lax.rem(k * 13, PEERS)

    def start(k, carry):
        rows(order(k)).start()
        if with_ids:
            numbers(order(k)).start()
        return carry

    def wait(k, carry):
        rows(k).wait()
        if with_ids:
            numbers(k).wait()
        return carry

    lax.fori_loop(1, PEERS, start, 0)
    own = pltpu.make_async_copy(x_ref.at[me], o_ref.at[me], here.at[0])
    own.start()
    if with_ids:
        own_ids = pltpu.make_async_copy(i_ref.at[me // 4], oi_ref.at[me], here.at[1])
        own_ids.start()
        own_ids.wait()
    own.wait()
    lax.fori_loop(1, PEERS, wait, 0)


def exchange(x, ids=None):
    with_ids = ids is not None
    shape = jax.ShapeDtypeStruct((PEERS, EACH, D), BF16)
    sems = [pltpu.SemaphoreType.DMA((PEERS,))] * (4 if with_ids else 2)
    sems = sems + [pltpu.SemaphoreType.DMA((2,))]
    args = (x.reshape(PEERS, EACH, D),)
    out_shape = shape
    out_specs = vmem(1)[0]
    if with_ids:
        args = args + (ids,)
        out_shape = [shape, jax.ShapeDtypeStruct((PEERS, 1, 128), jnp.int32)]
        out_specs = vmem(2)
    return pl.pallas_call(
        functools.partial(exchange_kernel, with_ids),
        in_specs=vmem(len(args)),
        out_specs=out_specs,
        out_shape=out_shape,
        scratch_shapes=sems,
        compiler_params=pltpu.CompilerParams(
            collective_id=0 if with_ids else 1, has_side_effects=True),
        name="exchange_ids" if with_ids else "exchange",
    )(*args)


def place_kernel(row_ref, x_ref, gain_ref, grouped_ref, normed_ref, pooled_ref):
    hot = one_hot_rows(pl.program_id(0) * 256, 256, row_ref[...])
    rows = mm(hot, x_ref[...])
    grouped_ref[...] = rows.astype(BF16)
    mean = jnp.mean(rows * rows, axis=-1, keepdims=True)
    normed = (rows * lax.rsqrt(mean + 1e-5) * gain_ref[...]).astype(BF16)
    normed_ref[...] = normed
    r = lax.broadcasted_iota(jnp.int32, (CK, BALL), 0)
    c = lax.broadcasted_iota(jnp.int32, (CK, BALL), 1)
    pool = jnp.where(c // POOL == r, 1.0 / POOL, 0.0).astype(BF16)
    pooled_ref[...] = mm(pool, normed).astype(BF16)


def place(row, x, gain):
    return pl.pallas_call(
        place_kernel,
        grid=(NB,),
        in_specs=[fixed((1, ROWS)), fixed((ROWS, D)), fixed((1, D))],
        out_specs=[
            pl.BlockSpec((BALL, D), lambda i: (i, 0)),
            pl.BlockSpec((BALL, D), lambda i: (i, 0)),
            pl.BlockSpec((CK, D), lambda i: (i, 0)),
        ],
        out_shape=[
            jax.ShapeDtypeStruct((ROWS, D), BF16),
            jax.ShapeDtypeStruct((ROWS, D), BF16),
            jax.ShapeDtypeStruct((NB * CK, D), BF16),
        ],
        compiler_params=pltpu.CompilerParams(vmem_limit_bytes=VMEM_LIMIT),
        name="place",
    )(row, x, gain)


def head_norm_cols(u):
    shaped = u.reshape(HEADS, HD, u.shape[1])
    mean = jnp.mean(shaped * shaped, axis=1, keepdims=True)
    return (shaped * lax.rsqrt(mean + 1e-6)).astype(BF16)


def layer_kernel(
    chosen_ref, normed_ref, grouped_ref, cand_ref, wq_ref, wk_ref, wv_ref, wpk_ref,
    wpv_ref, wo_ref, wg_ref, wu_ref, wd_ref, scale_ref, gain_ref, mix_ref, sum_ref,
    out_ref, keys, values, probs, partial,
):
    ball = pl.program_id(0)

    @pl.when(ball == 0)
    def _():
        keys[...] = jnp.zeros_like(keys)
        values[...] = jnp.zeros_like(values)

    normed = normed_ref[...]
    q = mm(normed, wq_ref[...])
    square = (q * q).astype(BF16)
    mean = jnp.concatenate(
        [mm(square[:, :256], mix_ref[...]), mm(square[:, 256:], mix_ref[...])], axis=1)
    query = (q * lax.rsqrt(mean + 1e-6) * scale_ref[...]).astype(BF16)
    near_key = head_norm_cols(mm_nt(wk_ref[...], normed))
    near_value = mm(normed, wv_ref[...]).astype(BF16)
    picked = jnp.concatenate(
        [cand_ref[pl.ds(pl.multiple_of(chosen_ref[ball, j] * CK, CK), CK), :]
         for j in range(OWNERS)], axis=0)
    far_key = head_norm_cols(mm_nt(wpk_ref[...], picked))
    far_value = mm(picked, wpv_ref[...]).astype(BF16)
    lane = lax.broadcasted_iota(jnp.int32, (1, 128), 1) // HD
    for h in range(HEADS):
        g, l = h // GROUP, h % GROUP
        at = l * KEYS
        r = slice(l * HD, (l + 1) * HD)
        keys[g, r, at:at + BALL] = near_key[h]
        keys[g, r, at + BALL:at + KEYS] = far_key[h]
        t = l // 4
        cols = slice(g * 256 + t * 128, g * 256 + t * 128 + 128)
        mask = lane == (l % 4)
        zero = jnp.zeros((), BF16)
        values[g, at:at + BALL, t * 128:(t + 1) * 128] = jnp.where(
            mask, near_value[:, cols], zero)
        values[g, at + BALL:at + KEYS, t * 128:(t + 1) * 128] = jnp.where(
            mask, far_value[:, cols], zero)
    attended = []
    for g in range(HEADS // GROUP):
        qg = query[:, g * 256:(g + 1) * 256]
        for l in range(GROUP):
            p = jnp.exp2(mm(qg, keys[g, :, l * KEYS:(l + 1) * KEYS]))
            probs[:, l * KEYS:(l + 1) * KEYS] = p.astype(BF16)
            partial[:, l * 128:(l + 1) * 128] = (
                p[:, :128] + p[:, 128:256] + p[:, 256:384]).astype(BF16)
        total = mm(probs[...], values[g])
        denominator = mm(partial[...], sum_ref[...])
        attended.append((total / denominator).astype(BF16))
    attended = jnp.concatenate(attended, axis=1)
    residual = (grouped_ref[...].astype(F32) + mm(attended, wo_ref[...])).astype(BF16)
    wide = residual.astype(F32)
    mean = jnp.mean(wide * wide, axis=-1, keepdims=True)
    ffn = (wide * lax.rsqrt(mean + 1e-5) * gain_ref[...]).astype(BF16)
    gate = mm(ffn, wg_ref[...])
    up = mm(ffn, wu_ref[...])
    hidden = (gate / (1.0 + jnp.exp(-gate)) * up).astype(BF16)
    out_ref[...] = (wide + mm(hidden, wd_ref[...])).astype(BF16)


def layer(chosen, normed, grouped, cand, weights):
    rows = pl.BlockSpec((BALL, D), lambda i, _: (i, 0))
    return pl.pallas_call(
        layer_kernel,
        grid_spec=pltpu.PrefetchScalarGridSpec(
            num_scalar_prefetch=1,
            grid=(NB,),
            in_specs=[rows, rows, fixed(cand.shape)] + [fixed(w.shape) for w in weights],
            out_specs=rows,
            scratch_shapes=[
                pltpu.VMEM((2, 256, GROUP * KEYS), BF16),
                pltpu.VMEM((2, GROUP * KEYS, 256), BF16),
                pltpu.VMEM((BALL, GROUP * KEYS), BF16),
                pltpu.VMEM((BALL, GROUP * 128), BF16),
            ],
        ),
        out_shape=jax.ShapeDtypeStruct((ROWS, D), BF16),
        compiler_params=pltpu.CompilerParams(vmem_limit_bytes=VMEM_LIMIT),
        name="layer",
    )(chosen, normed, grouped, cand, *weights)


def pick_kernel(col_ref, x_ref, out_ref):
    hot = one_hot_cols(col_ref[...], 256)
    out_ref[...] = mm(hot, x_ref[...]).astype(BF16)


def pick(col, x):
    return pl.pallas_call(
        pick_kernel,
        grid=(NB,),
        in_specs=[pl.BlockSpec((256, 1), lambda i: (i, 0)), fixed((ROWS, D))],
        out_specs=pl.BlockSpec((256, D), lambda i: (i, 0)),
        out_shape=jax.ShapeDtypeStruct((ROWS, D), BF16),
        compiler_params=pltpu.CompilerParams(vmem_limit_bytes=VMEM_LIMIT),
        name="pick",
    )(col, x)


def from_behind(block, distance):
    route = [((i - distance) % PEERS, i) for i in range(PEERS)]
    return lax.ppermute(block, "pts", route)


def on_device(
    points, point_row_index, neighbour_ball_list, attention_norm_gain, query_weight,
    key_weight, value_weight, pooled_key_weight, pooled_value_weight, head_score_scale,
    output_weight, feedforward_norm_gain, gate_weight, up_weight, down_weight,
):
    me = lax.axis_index("pts")
    outgoing, ids, pos = pack(
        point_row_index.reshape(ROWS, 1), point_row_index.reshape(1, ROWS), points)
    arrived, all_ids = exchange(outgoing, ids)
    mine = lax.dynamic_slice_in_dim(all_ids.reshape(PEERS, 128), (me % 4) * EACH, EACH, 1)
    slot = mine.reshape(ROWS) - me * ROWS
    grouped, normed, pooled = place(
        slot.reshape(1, ROWS), arrived.reshape(ROWS, D), attention_norm_gain.reshape(1, D))
    blocks = [from_behind(pooled, k) if k else pooled for k in range(REACH, -REACH - 1, -1)]
    cand = jnp.concatenate(blocks, axis=0)
    owner = neighbour_ball_list // NB
    offset = jnp.mod(owner - me + REACH, PEERS)
    chosen = offset * NB + neighbour_ball_list % NB
    scale = jnp.repeat(head_score_scale * (math.log2(math.e) / HD), HD).reshape(1, D)
    a = lax.broadcasted_iota(jnp.int32, (256, 256), 0) // HD
    b = lax.broadcasted_iota(jnp.int32, (256, 256), 1) // HD
    mix = jnp.where(a == b, 1.0 / HD, 0.0).astype(BF16)
    a = lax.broadcasted_iota(jnp.int32, (GROUP * 128, 256), 0) // 128
    b = lax.broadcasted_iota(jnp.int32, (GROUP * 128, 256), 1) // HD
    spread = jnp.where(a == b, 1.0, 0.0).astype(BF16)
    ball_out = layer(
        chosen, normed, grouped, cand,
        (query_weight, key_weight.T, value_weight, pooled_key_weight.T, pooled_value_weight,
         output_weight, gate_weight, up_weight, down_weight, scale,
         feedforward_norm_gain.reshape(1, D), mix, spread))
    returning = pick(slot.reshape(ROWS, 1), ball_out)
    came_back = exchange(returning)
    return pick(pos.reshape(ROWS, 1), came_back.reshape(ROWS, D))


def solution(mesh):
    return jax.shard_map(
        on_device,
        mesh=mesh,
        in_specs=(
            P(("rep", "pts"), None), P(("rep", "pts")), P(("rep", "pts"), None),
            P(), P(), P(), P(), P(), P(), P(), P(), P(), P(), P(), P(),
        ),
        out_specs=P(("rep", "pts"), None),
        check_vma=False,
    )
```

```python
import functools
import math

import jax
import jax.numpy as jnp
from jax import lax
from jax.experimental import pallas as pl
from jax.experimental.pallas import tpu as pltpu
from jax.sharding import PartitionSpec as P

BALL = 256
POOL = 8
OWNERS = 4
D = 512
HEADS = 16
HD = 32
FF = 1024
ROWS = 2048
PEERS = 64
EACH = 32
CK = BALL // POOL
KEYS = BALL + OWNERS * CK
GROUP = 8
NB = ROWS // BALL
CHIPS = PEERS // 2
MESH = pl.DeviceIdType.MESH
F32 = jnp.float32
BF16 = jnp.bfloat16
VMEM_LIMIT = 56 * 1024 * 1024


def vmem(n):
    return [pl.BlockSpec(memory_space=pltpu.VMEM)] * n


def fixed(shape):
    return pl.BlockSpec(shape, lambda *_: (0,) * len(shape), pipeline_mode=pl.Buffered(1))


def mm(a, b):
    return jnp.dot(a, b, preferred_element_type=F32)


def mm_nt(a, b):
    return lax.dot_general(a, b, (((1,), (1,)), ((), ())), preferred_element_type=F32)


def one_hot_rows(start, count, row):
    ids = lax.broadcasted_iota(jnp.int32, (count, ROWS), 0) + start
    return jnp.where(ids == row, 1.0, 0.0).astype(BF16)


def one_hot_cols(col, count):
    ids = lax.broadcasted_iota(jnp.int32, (count, ROWS), 1)
    return jnp.where(ids == col, 1.0, 0.0).astype(BF16)


def pack_kernel(col_ref, row_ref, x_ref, out_ref, ids_ref, pos_ref):
    step = pl.program_id(0)

    @pl.when(step == 0)
    def _():
        def count(j, acc):
            col = col_ref[pl.ds(pl.multiple_of(j * 256, 256), 256), :]
            less = jnp.where(col < row_ref[...], 1.0, 0.0)
            return acc + jnp.sum(less.reshape(32, 8, ROWS), axis=0)

        acc = lax.fori_loop(0, NB, count, jnp.zeros((8, ROWS), F32))
        pos_ref[...] = jnp.sum(acc, axis=0, keepdims=True).astype(jnp.int32)

    hot = one_hot_rows(step * 256, 256, pos_ref[...])
    out_ref[...] = mm(hot, x_ref[...]).astype(BF16)
    number = row_ref[...]
    high = (number // 2048).astype(F32)
    mid = ((number // 64) % 32).astype(F32)
    low = (number % 64).astype(F32)
    pad = jnp.zeros((5, ROWS), F32)
    parts = jnp.concatenate([high, mid, low, pad], axis=0).astype(BF16)
    back = mm_nt(parts, hot)
    whole = back[0:1] * 2048.0 + back[1:2] * 64.0 + back[2:3]
    whole = whole.astype(jnp.int32)
    ids_ref[0] = whole[:, :128]
    ids_ref[1] = whole[:, 128:]


def pack(col, row, x):
    return pl.pallas_call(
        pack_kernel,
        grid=(NB,),
        in_specs=[fixed((ROWS, 1)), fixed((1, ROWS)), fixed((ROWS, D))],
        out_specs=[
            pl.BlockSpec((256, D), lambda i: (i, 0)),
            pl.BlockSpec((2, 1, 128), lambda i: (i, 0, 0)),
            pl.BlockSpec((1, ROWS), lambda i: (0, 0)),
        ],
        out_shape=[
            jax.ShapeDtypeStruct((ROWS, D), BF16),
            jax.ShapeDtypeStruct((16, 1, 128), jnp.int32),
            jax.ShapeDtypeStruct((1, ROWS), jnp.int32),
        ],
        compiler_params=pltpu.CompilerParams(vmem_limit_bytes=VMEM_LIMIT),
        name="pack",
    )(col, row, x)


def peer(k):
    return lax.rem(lax.axis_index("pts") + k, PEERS)


def greet():
    barrier = pltpu.get_barrier_semaphore()

    def signal(k, carry):
        pl.semaphore_signal(barrier, inc=1, device_id={"pts": peer(k)}, device_id_type=MESH)
        return carry

    lax.fori_loop(1, PEERS, signal, 0)
    pl.semaphore_wait(barrier, PEERS - 1)


def exchange_kernel(with_ids, *refs):
    if with_ids:
        x_ref, i_ref, o_ref, oi_ref, send, recv, isend, irecv, here = refs
    else:
        x_ref, o_ref, send, recv, here = refs
    me = lax.axis_index("pts")
    greet()

    def rows(k):
        d = peer(k)
        return pltpu.make_async_remote_copy(
            src_ref=x_ref.at[d], dst_ref=o_ref.at[me], send_sem=send.at[k],
            recv_sem=recv.at[k], device_id={"pts": d}, device_id_type=MESH)

    def numbers(k):
        d = peer(k)
        return pltpu.make_async_remote_copy(
            src_ref=i_ref.at[d // 4], dst_ref=oi_ref.at[me], send_sem=isend.at[k],
            recv_sem=irecv.at[k], device_id={"pts": d}, device_id_type=MESH)

    def order(k):
        return lax.rem(k * 13, PEERS)

    def start(k, carry):
        rows(order(k)).start()
        if with_ids:
            numbers(order(k)).start()
        return carry

    def wait(k, carry):
        rows(k).wait()
        if with_ids:
            numbers(k).wait()
        return carry

    lax.fori_loop(1, PEERS, start, 0)
    own = pltpu.make_async_copy(x_ref.at[me], o_ref.at[me], here.at[0])
    own.start()
    if with_ids:
        own_ids = pltpu.make_async_copy(i_ref.at[me // 4], oi_ref.at[me], here.at[1])
        own_ids.start()
        own_ids.wait()
    own.wait()
    lax.fori_loop(1, PEERS, wait, 0)


def exchange(x, ids=None):
    with_ids = ids is not None
    shape = jax.ShapeDtypeStruct((PEERS, EACH, D), BF16)
    sems = [pltpu.SemaphoreType.DMA((PEERS,))] * (4 if with_ids else 2)
    sems = sems + [pltpu.SemaphoreType.DMA((2,))]
    args = (x.reshape(PEERS, EACH, D),)
    out_shape = shape
    out_specs = vmem(1)[0]
    if with_ids:
        args = args + (ids,)
        out_shape = [shape, jax.ShapeDtypeStruct((PEERS, 1, 128), jnp.int32)]
        out_specs = vmem(2)
    return pl.pallas_call(
        functools.partial(exchange_kernel, with_ids),
        in_specs=vmem(len(args)),
        out_specs=out_specs,
        out_shape=out_shape,
        scratch_shapes=sems,
        compiler_params=pltpu.CompilerParams(
            collective_id=0 if with_ids else 1, has_side_effects=True),
        name="exchange_ids" if with_ids else "exchange",
    )(*args)


def place_kernel(row_ref, x_ref, gain_ref, grouped_ref, normed_ref, pooled_ref):
    hot = one_hot_rows(pl.program_id(0) * 256, 256, row_ref[...])
    rows = mm(hot, x_ref[...])
    grouped_ref[...] = rows.astype(BF16)
    mean = jnp.mean(rows * rows, axis=-1, keepdims=True)
    normed = (rows * lax.rsqrt(mean + 1e-5) * gain_ref[...]).astype(BF16)
    normed_ref[...] = normed
    r = lax.broadcasted_iota(jnp.int32, (CK, BALL), 0)
    c = lax.broadcasted_iota(jnp.int32, (CK, BALL), 1)
    pool = jnp.where(c // POOL == r, 1.0 / POOL, 0.0).astype(BF16)
    pooled_ref[...] = mm(pool, normed).astype(BF16)


def place(row, x, gain):
    return pl.pallas_call(
        place_kernel,
        grid=(NB,),
        in_specs=[fixed((1, ROWS)), fixed((ROWS, D)), fixed((1, D))],
        out_specs=[
            pl.BlockSpec((BALL, D), lambda i: (i, 0)),
            pl.BlockSpec((BALL, D), lambda i: (i, 0)),
            pl.BlockSpec((CK, D), lambda i: (i, 0)),
        ],
        out_shape=[
            jax.ShapeDtypeStruct((ROWS, D), BF16),
            jax.ShapeDtypeStruct((ROWS, D), BF16),
            jax.ShapeDtypeStruct((NB * CK, D), BF16),
        ],
        compiler_params=pltpu.CompilerParams(vmem_limit_bytes=VMEM_LIMIT),
        name="place",
    )(row, x, gain)


def head_norm_cols(u):
    shaped = u.reshape(HEADS, HD, u.shape[1])
    mean = jnp.mean(shaped * shaped, axis=1, keepdims=True)
    return (shaped * lax.rsqrt(mean + 1e-6)).astype(BF16)


def block_ones(rows, per_row, per_col, value):
    a = lax.broadcasted_iota(jnp.int32, (rows, 256), 0) // per_row
    b = lax.broadcasted_iota(jnp.int32, (rows, 256), 1) // per_col
    return jnp.where(a == b, value, 0.0).astype(BF16)


def set_heads(keys, values, key, value, count):
    lane = lax.broadcasted_iota(jnp.int32, (1, 128), 1) // HD
    zero = jnp.zeros((), BF16)
    for h in range(HEADS):
        g, l = h // GROUP, h % GROUP
        t = l // 4
        at = slice(l * count, (l + 1) * count)
        keys[g, l * HD:(l + 1) * HD, at] = key[h]
        cols = slice(g * 256 + t * 128, g * 256 + t * 128 + 128)
        values[g, at, t * 128:(t + 1) * 128] = jnp.where(lane == (l % 4), value[:, cols], zero)


def attention_kernel(
    chosen_ref, normed_ref, grouped_ref, pooled_ref, wq_ref, wk_ref, wv_ref, wpk_ref,
    wpv_ref, wo_ref, scale_ref, out_ref,
    cand, near_keys, near_values, far_keys, far_values, probs, partial, queries,
    totals, sums, wk_t, wpk_t, mix, spread, send, recv, here,
):
    me = lax.axis_index("pts")
    core = me % 2
    chip = me // 2
    partner = chip * 2 + 1 - core
    steps = (1, -1, 2, -2)

    def chip_at(e):
        return ((chip + e + CHIPS) % CHIPS) * 2 + core

    barrier = pltpu.get_barrier_semaphore()
    for d in [partner] + [chip_at(e) for e in steps]:
        pl.semaphore_signal(barrier, inc=1, device_id={"pts": d}, device_id_type=MESH)
    pl.semaphore_wait(barrier, 1 + len(steps))

    def block(slot):
        return cand.at[pl.ds(slot * NB, NB)]

    def remote(src, slot, at, d):
        return pltpu.make_async_remote_copy(
            src_ref=src, dst_ref=block(slot), send_sem=send.at[at], recv_sem=recv.at[at],
            device_id={"pts": d}, device_id_type=MESH)

    outs = [remote(pooled_ref, (2 - e) * 2 + core, 1 + i, chip_at(e))
            for i, e in enumerate(steps)]
    for copy in outs:
        copy.start()
    to_partner = remote(pooled_ref, 4 + core, 0, partner)
    to_partner.start()
    own = pltpu.make_async_copy(pooled_ref, block(4 + core), here.at[0])
    own.start()
    onward = [remote(block((2 - e) * 2 + core), (2 - e) * 2 + core, 5 + i, partner)
              for i, e in enumerate(steps)]

    for ref in (near_keys, near_values, far_keys, far_values):
        ref[...] = jnp.zeros_like(ref)
    wk_t[...] = wk_ref[...].T
    wpk_t[...] = wpk_ref[...].T
    mix[...] = block_ones(256, HD, HD, 1.0 / HD)
    spread[...] = block_ones(GROUP * 128, 128, HD, 1.0)

    def near(ball, carry):
        for at, pair in ((5, (0, 1)), (7, (2, 3))):
            @pl.when(ball == at)
            def _():
                for i in pair:
                    outs[i].wait_recv()
                    onward[i].start()

        rows = pl.ds(pl.multiple_of(ball * BALL, BALL), BALL)
        normed = normed_ref[rows, :]
        q = mm(normed, wq_ref[...])
        square = (q * q).astype(BF16)
        mean = jnp.concatenate(
            [mm(square[:, :256], mix[...]), mm(square[:, 256:], mix[...])], axis=1)
        query = (q * lax.rsqrt(mean + 1e-6) * scale_ref[...]).astype(BF16)
        queries[rows, :] = query
        key = head_norm_cols(mm_nt(wk_t[...], normed))
        value = mm(normed, wv_ref[...]).astype(BF16)
        set_heads(near_keys, near_values, key, value, BALL)
        for g in range(HEADS // GROUP):
            cols = slice(g * 256, (g + 1) * 256)
            qg = query[:, cols]
            for l in range(GROUP):
                p = jnp.exp2(mm(qg, near_keys[g, :, l * BALL:(l + 1) * BALL]))
                probs[:, l * BALL:(l + 1) * BALL] = p.astype(BF16)
                partial[:, l * 128:(l + 1) * 128] = (p[:, :128] + p[:, 128:]).astype(BF16)
            totals[rows, cols] = mm(probs[...], near_values[g])
            sums[rows, cols] = mm(partial[...], spread[...])
        return carry

    lax.fori_loop(0, NB, near, 0)
    own.wait()
    to_partner.wait()
    for copy in outs:
        copy.wait_send()
    for copy in onward:
        copy.wait()

    def far(ball, carry):
        rows = pl.ds(pl.multiple_of(ball * BALL, BALL), BALL)
        picked = []
        for j in range(OWNERS):
            picked.append(cand[chosen_ref[ball, j]])
        picked = jnp.concatenate(picked, axis=0)
        key = head_norm_cols(mm_nt(wpk_t[...], picked))
        value = mm(picked, wpv_ref[...]).astype(BF16)
        set_heads(far_keys, far_values, key, value, OWNERS * CK)
        attended = []
        for g in range(HEADS // GROUP):
            cols = slice(g * 256, (g + 1) * 256)
            qg = queries[rows, cols]
            for l in range(GROUP // 2):
                p = jnp.exp2(mm(qg, far_keys[g, :, l * 256:(l + 1) * 256]))
                partial[:, l * 256:(l + 1) * 256] = p.astype(BF16)
            total = totals[rows, cols] + mm(partial[...], far_values[g])
            denominator = sums[rows, cols] + mm(partial[...], spread[...])
            attended.append((total / denominator).astype(BF16))
        attended = jnp.concatenate(attended, axis=1)
        out_ref[rows, :] = (
            grouped_ref[rows, :].astype(F32) + mm(attended, wo_ref[...])).astype(BF16)
        return carry

    lax.fori_loop(0, NB, far, 0)


def attention(chosen, arrays):
    return pl.pallas_call(
        attention_kernel,
        in_specs=[pl.BlockSpec(memory_space=pltpu.SMEM)] + vmem(len(arrays)),
        out_specs=vmem(1)[0],
        out_shape=jax.ShapeDtypeStruct((ROWS, D), BF16),
        scratch_shapes=[
            pltpu.VMEM((10 * NB, CK, D), BF16),
            pltpu.VMEM((2, 256, GROUP * BALL), BF16),
            pltpu.VMEM((2, GROUP * BALL, 256), BF16),
            pltpu.VMEM((2, 256, GROUP * 128), BF16),
            pltpu.VMEM((2, GROUP * 128, 256), BF16),
            pltpu.VMEM((BALL, GROUP * BALL), BF16),
            pltpu.VMEM((BALL, GROUP * 128), BF16),
            pltpu.VMEM((ROWS, D), BF16),
            pltpu.VMEM((ROWS, D), F32),
            pltpu.VMEM((ROWS, D), F32),
            pltpu.VMEM((D, D), BF16),
            pltpu.VMEM((D, D), BF16),
            pltpu.VMEM((256, 256), BF16),
            pltpu.VMEM((GROUP * 128, 256), BF16),
            pltpu.SemaphoreType.DMA((9,)),
            pltpu.SemaphoreType.DMA((9,)),
            pltpu.SemaphoreType.DMA((1,)),
        ],
        compiler_params=pltpu.CompilerParams(
            collective_id=2, has_side_effects=True, vmem_limit_bytes=VMEM_LIMIT),
        name="attention",
    )(chosen, *arrays)


def finish_kernel(col_ref, res_ref, wg_ref, wu_ref, wd_ref, gain_ref, out_ref,
                  ready, send, recv, here):
    me = lax.axis_index("pts")
    greet()

    def back(k):
        d = peer((k * 13) % PEERS)
        return pltpu.make_async_remote_copy(
            src_ref=ready.at[k], dst_ref=out_ref.at[me], send_sem=send.at[k],
            recv_sem=recv.at[k], device_id={"pts": d}, device_id_type=MESH)

    own = pltpu.make_async_copy(ready.at[0], out_ref.at[me], here.at[0])

    def start(k, carry):
        @pl.when(k > 0)
        def _():
            back(k).start()

        @pl.when(k == 0)
        def _():
            own.start()
        return carry

    def chunk(c, carry):
        cols = [col_ref[pl.ds(pl.multiple_of(peer(((c * 8 + j) * 13) % PEERS) * EACH, EACH),
                              EACH), :] for j in range(8)]
        hot = one_hot_cols(jnp.concatenate(cols, axis=0), 256)
        wide = mm(hot, res_ref[...])
        mean = jnp.mean(wide * wide, axis=-1, keepdims=True)
        ffn = (wide * lax.rsqrt(mean + 1e-5) * gain_ref[...]).astype(BF16)
        gate = mm(ffn, wg_ref[...])
        up = mm(ffn, wu_ref[...])
        hidden = (gate / (1.0 + jnp.exp(-gate)) * up).astype(BF16)
        result = (wide + mm(hidden, wd_ref[...])).astype(BF16)
        ready[pl.ds(pl.multiple_of(c * 8, 8), 8)] = result.reshape(8, EACH, D)

        @pl.when(c > 0)
        def _():
            lax.fori_loop(c * 8 - 8, c * 8, start, 0)
        return carry

    lax.fori_loop(0, NB, chunk, 0)
    lax.fori_loop(PEERS - 8, PEERS, start, 0)

    def wait(k, carry):
        back(k).wait()
        return carry

    own.wait()
    lax.fori_loop(1, PEERS, wait, 0)


def finish(*arrays):
    return pl.pallas_call(
        finish_kernel,
        in_specs=vmem(len(arrays)),
        out_specs=vmem(1)[0],
        out_shape=jax.ShapeDtypeStruct((PEERS, EACH, D), BF16),
        scratch_shapes=[
            pltpu.VMEM((PEERS, EACH, D), BF16),
            pltpu.SemaphoreType.DMA((PEERS,)),
            pltpu.SemaphoreType.DMA((PEERS,)),
            pltpu.SemaphoreType.DMA((1,)),
        ],
        compiler_params=pltpu.CompilerParams(
            collective_id=1, has_side_effects=True, vmem_limit_bytes=VMEM_LIMIT),
        name="finish",
    )(*arrays)


def pick_kernel(col_ref, x_ref, out_ref):
    hot = one_hot_cols(col_ref[...], 256)
    out_ref[...] = mm(hot, x_ref[...]).astype(BF16)


def pick(col, x):
    return pl.pallas_call(
        pick_kernel,
        grid=(NB,),
        in_specs=[pl.BlockSpec((256, 1), lambda i: (i, 0)), fixed((ROWS, D))],
        out_specs=pl.BlockSpec((256, D), lambda i: (i, 0)),
        out_shape=jax.ShapeDtypeStruct((ROWS, D), BF16),
        compiler_params=pltpu.CompilerParams(vmem_limit_bytes=VMEM_LIMIT),
        name="pick",
    )(col, x)


def on_device(
    points, point_row_index, neighbour_ball_list, attention_norm_gain, query_weight,
    key_weight, value_weight, pooled_key_weight, pooled_value_weight, head_score_scale,
    output_weight, feedforward_norm_gain, gate_weight, up_weight, down_weight,
):
    me = lax.axis_index("pts")
    outgoing, ids, pos = pack(
        point_row_index.reshape(ROWS, 1), point_row_index.reshape(1, ROWS), points)
    arrived, all_ids = exchange(outgoing, ids)
    mine = lax.dynamic_slice_in_dim(all_ids.reshape(PEERS, 128), (me % 4) * EACH, EACH, 1)
    slot = mine.reshape(ROWS) - me * ROWS
    grouped, normed, pooled = place(
        slot.reshape(1, ROWS), arrived.reshape(ROWS, D), attention_norm_gain.reshape(1, D))
    owner = neighbour_ball_list // NB
    place_of = jnp.mod(owner // 2 - me // 2 + 2, CHIPS) * 2 + owner % 2
    chosen = place_of * NB + neighbour_ball_list % NB
    scale = jnp.repeat(head_score_scale * (math.log2(math.e) / HD), HD).reshape(1, D)
    residual = attention(
        chosen,
        (normed, grouped, pooled.reshape(NB, CK, D), query_weight, key_weight, value_weight, pooled_key_weight,
         pooled_value_weight, output_weight, scale))
    came_back = finish(slot.reshape(ROWS, 1), residual, gate_weight, up_weight, down_weight,
                       feedforward_norm_gain.reshape(1, D))
    return pick(pos.reshape(ROWS, 1), came_back.reshape(ROWS, D))


def solution(mesh):
    return jax.shard_map(
        on_device,
        mesh=mesh,
        in_specs=(
            P(("rep", "pts"), None), P(("rep", "pts")), P(("rep", "pts"), None),
            P(), P(), P(), P(), P(), P(), P(), P(), P(), P(), P(), P(),
        ),
        out_specs=P(("rep", "pts"), None),
        check_vma=False,
    )
```

```python
import functools
import math

import jax
import jax.numpy as jnp
from jax import lax
from jax.experimental import pallas as pl
from jax.experimental.pallas import tpu as pltpu
from jax.sharding import PartitionSpec as P

BALL = 256
POOL = 8
OWNERS = 4
D = 512
HEADS = 16
HD = 32
FF = 1024
ROWS = 2048
PEERS = 64
EACH = 32
CK = BALL // POOL
KEYS = BALL + OWNERS * CK
GROUP = 8
NB = ROWS // BALL
STRIDE = 13
INVERSE = 5
CHIPS = PEERS // 2
MESH = pl.DeviceIdType.MESH
F32 = jnp.float32
BF16 = jnp.bfloat16
VMEM_LIMIT = 56 * 1024 * 1024


def vmem(n):
    return [pl.BlockSpec(memory_space=pltpu.VMEM)] * n


def mm(a, b):
    return jnp.dot(a, b, preferred_element_type=F32)


def mm_nt(a, b):
    return lax.dot_general(a, b, (((1,), (1,)), ((), ())), preferred_element_type=F32)


def one_hot_rows(start, count, row):
    ids = lax.broadcasted_iota(jnp.int32, (count, row.shape[1]), 0) + start
    return jnp.where(ids == row, 1.0, 0.0).astype(BF16)


def one_hot_cols(start, col, width):
    ids = lax.broadcasted_iota(jnp.int32, (col.shape[0], width), 1) + start
    return jnp.where(ids == col, 1.0, 0.0).astype(BF16)


def column(row):
    wide = jnp.broadcast_to(row.astype(F32), (8, row.shape[1]))
    return wide.T[:, :1].astype(jnp.int32)


def ahead(k):
    return (lax.axis_index("pts") + STRIDE * k) % PEERS


def behind(k):
    return (lax.axis_index("pts") + PEERS * STRIDE - STRIDE * k) % PEERS


def greet():
    barrier = pltpu.get_barrier_semaphore()

    def signal(k, carry):
        pl.semaphore_signal(barrier, inc=1, device_id={"pts": ahead(k)}, device_id_type=MESH)
        return carry

    lax.fori_loop(1, PEERS, signal, 0)


def met():
    pl.semaphore_wait(pltpu.get_barrier_semaphore(), PEERS - 1)


def steps(lo, hi, body):
    def step(k, carry):
        body(k)
        return carry

    lax.fori_loop(lo, hi, step, 0)


def front_kernel(
    row_ref, x_ref, gain_ref, grouped_ref, normed_ref, pooled_ref, pos_ref, slot_ref,
    col, ready, numbers, landed, landed_numbers, send, recv, nsend, nrecv, here,
):
    me = lax.axis_index("pts")
    greet()
    row = row_ref[...]
    col[...] = column(row)

    def count(j, acc):
        part = col[pl.ds(pl.multiple_of(j * 256, 256), 256), :]
        less = jnp.where(part < row, 1.0, 0.0)
        return acc + jnp.sum(less.reshape(32, 8, ROWS), axis=0)

    acc = lax.fori_loop(0, NB, count, jnp.zeros((8, ROWS), F32))
    rank = jnp.sum(acc, axis=0, keepdims=True).astype(jnp.int32)
    turn = (((rank >> 5) + PEERS - me) * INVERSE) & (PEERS - 1)
    pos_ref[...] = turn * EACH + (rank & (EACH - 1))
    slot = row & (ROWS - 1)
    parts = jnp.concatenate(
        [(slot >> 6).astype(F32), (slot & 63).astype(F32), jnp.zeros((6, ROWS), F32)],
        axis=0).astype(BF16)

    def rows(k):
        return pltpu.make_async_remote_copy(
            src_ref=ready.at[k], dst_ref=landed.at[k], send_sem=send.at[k],
            recv_sem=recv.at[k], device_id={"pts": ahead(k)}, device_id_type=MESH)

    def ids(k):
        return pltpu.make_async_remote_copy(
            src_ref=numbers.at[k // 4], dst_ref=landed_numbers.at[k], send_sem=nsend.at[k],
            recv_sem=nrecv.at[k], device_id={"pts": ahead(k)}, device_id_type=MESH)

    def start(k):
        ids(k).start()
        rows(k).start()

    def prepare(c):
        hot = one_hot_rows(c * 256, 256, pos_ref[...])
        ready[pl.ds(pl.multiple_of(c * 8, 8), 8)] = mm(hot, x_ref[...]).astype(BF16).reshape(
            8, EACH, D)
        back = mm_nt(parts, hot)
        whole = (back[0:1] * 64.0 + back[1:2]).astype(jnp.int32)
        numbers[2 * c] = whole[:, :128]
        numbers[2 * c + 1] = whole[:, 128:]

    prepare(0)
    met()
    own = pltpu.make_async_copy(ready.at[0], landed.at[0], here.at[0])
    own_ids = pltpu.make_async_copy(numbers.at[0], landed_numbers.at[0], here.at[1])

    def more(c):
        prepare(c)
        first = c * 8 - 8
        steps(jnp.maximum(first, 1), first + 8, start)

    steps(1, NB, more)
    own.start()
    own_ids.start()
    steps(PEERS - 8, PEERS, start)
    own.wait()
    own_ids.wait()

    def place(c, first):
        def arrive(k):
            ids(k).wait_recv()
            rows(k).wait_recv()

        steps(1 if first else c * 8, c * 8 + 8, arrive)
        got = landed_numbers[pl.ds(pl.multiple_of(c * 8, 8), 8)]
        lane = lax.broadcasted_iota(jnp.int32, got.shape, 2) // EACH
        turn = lax.broadcasted_iota(jnp.int32, got.shape, 0) & 3
        got = jnp.where(lane == turn, got, 0)
        halves = [got[0] + got[1] + got[2] + got[3], got[4] + got[5] + got[6] + got[7]]
        number = jnp.concatenate(halves, axis=1)
        slot_ref[c] = number
        chunk = landed[pl.ds(pl.multiple_of(c * 8, 8), 8)].reshape(256, D)
        for b in range(NB):
            at = slice(b * BALL, (b + 1) * BALL)
            part = mm(one_hot_rows(b * BALL, BALL, number), chunk).astype(BF16)
            if first:
                grouped_ref[at, :] = part
            else:
                grouped_ref[at, :] = grouped_ref[at, :] + part

    place(0, True)
    steps(1, NB, lambda c: place(c, False))

    r = lax.broadcasted_iota(jnp.int32, (CK, BALL), 0)
    c = lax.broadcasted_iota(jnp.int32, (CK, BALL), 1)
    pool = jnp.where(c // POOL == r, 1.0 / POOL, 0.0).astype(BF16)

    def norm(b):
        at = pl.ds(pl.multiple_of(b * BALL, BALL), BALL)
        wide = grouped_ref[at, :].astype(F32)
        mean = jnp.mean(wide * wide, axis=-1, keepdims=True)
        normed = (wide * lax.rsqrt(mean + 1e-5) * gain_ref[...]).astype(BF16)
        normed_ref[at, :] = normed
        pooled_ref[b] = mm(pool, normed).astype(BF16)

    steps(0, NB, norm)

    def sent(k):
        ids(k).wait_send()
        rows(k).wait_send()

    steps(1, PEERS, sent)


def front(row, x, gain):
    return pl.pallas_call(
        front_kernel,
        in_specs=vmem(3),
        out_specs=vmem(5),
        out_shape=[
            jax.ShapeDtypeStruct((ROWS, D), BF16),
            jax.ShapeDtypeStruct((ROWS, D), BF16),
            jax.ShapeDtypeStruct((NB, CK, D), BF16),
            jax.ShapeDtypeStruct((1, ROWS), jnp.int32),
            jax.ShapeDtypeStruct((NB, 1, 256), jnp.int32),
        ],
        scratch_shapes=[
            pltpu.VMEM((ROWS, 1), jnp.int32),
            pltpu.VMEM((PEERS, EACH, D), BF16),
            pltpu.VMEM((16, 1, 128), jnp.int32),
            pltpu.VMEM((PEERS, EACH, D), BF16),
            pltpu.VMEM((PEERS, 1, 128), jnp.int32),
            pltpu.SemaphoreType.DMA((PEERS,)),
            pltpu.SemaphoreType.DMA((PEERS,)),
            pltpu.SemaphoreType.DMA((PEERS,)),
            pltpu.SemaphoreType.DMA((PEERS,)),
            pltpu.SemaphoreType.DMA((2,)),
        ],
        compiler_params=pltpu.CompilerParams(
            collective_id=0, has_side_effects=True, vmem_limit_bytes=VMEM_LIMIT),
        name="front",
    )(row, x, gain)


def head_norm_cols(u):
    shaped = u.reshape(HEADS, HD, u.shape[1])
    mean = jnp.mean(shaped * shaped, axis=1, keepdims=True)
    return (shaped * lax.rsqrt(mean + 1e-6)).astype(BF16)


def block_ones(rows, per_row, per_col, value):
    a = lax.broadcasted_iota(jnp.int32, (rows, 256), 0) // per_row
    b = lax.broadcasted_iota(jnp.int32, (rows, 256), 1) // per_col
    return jnp.where(a == b, value, 0.0).astype(BF16)


def set_heads(keys, values, key, value, count):
    lane = lax.broadcasted_iota(jnp.int32, (1, 128), 1) // HD
    zero = jnp.zeros((), BF16)
    for h in range(HEADS):
        g, l = h // GROUP, h % GROUP
        t = l // 4
        at = slice(l * count, (l + 1) * count)
        keys[g, l * HD:(l + 1) * HD, at] = key[h]
        cols = slice(g * 256 + t * 128, g * 256 + t * 128 + 128)
        values[g, at, t * 128:(t + 1) * 128] = jnp.where(lane == (l % 4), value[:, cols], zero)


def attention_kernel(
    chosen_ref, normed_ref, grouped_ref, pooled_ref, wq_ref, wk_ref, wv_ref, wpk_ref,
    wpv_ref, wo_ref, scale_ref, out_ref,
    cand, near_keys, near_values, far_keys, far_values, probs, partial, queries,
    totals, sums, wk_t, wpk_t, mix, spread, send, recv, here,
):
    me = lax.axis_index("pts")
    core = me % 2
    chip = me // 2
    partner = chip * 2 + 1 - core
    steps = (1, -1, 2, -2)

    def chip_at(e):
        return ((chip + e + CHIPS) % CHIPS) * 2 + core

    barrier = pltpu.get_barrier_semaphore()
    for d in [partner] + [chip_at(e) for e in steps]:
        pl.semaphore_signal(barrier, inc=1, device_id={"pts": d}, device_id_type=MESH)
    pl.semaphore_wait(barrier, 1 + len(steps))

    def block(slot):
        return cand.at[pl.ds(slot * NB, NB)]

    def remote(src, slot, at, d):
        return pltpu.make_async_remote_copy(
            src_ref=src, dst_ref=block(slot), send_sem=send.at[at], recv_sem=recv.at[at],
            device_id={"pts": d}, device_id_type=MESH)

    outs = [remote(pooled_ref, (2 - e) * 2 + core, 1 + i, chip_at(e))
            for i, e in enumerate(steps)]
    for copy in outs:
        copy.start()
    to_partner = remote(pooled_ref, 4 + core, 0, partner)
    to_partner.start()
    own = pltpu.make_async_copy(pooled_ref, block(4 + core), here.at[0])
    own.start()
    onward = [remote(block((2 - e) * 2 + core), (2 - e) * 2 + core, 5 + i, partner)
              for i, e in enumerate(steps)]

    for ref in (near_keys, near_values, far_keys, far_values):
        ref[...] = jnp.zeros_like(ref)
    wk_t[...] = wk_ref[...].T
    wpk_t[...] = wpk_ref[...].T
    mix[...] = block_ones(256, HD, HD, 1.0 / HD)
    spread[...] = block_ones(GROUP * 128, 128, HD, 1.0)

    def near(ball, carry):
        for at, pair in ((5, (0, 1)), (7, (2, 3))):
            @pl.when(ball == at)
            def _():
                for i in pair:
                    outs[i].wait_recv()
                    onward[i].start()

        rows = pl.ds(pl.multiple_of(ball * BALL, BALL), BALL)
        normed = normed_ref[rows, :]
        q = mm(normed, wq_ref[...])
        square = (q * q).astype(BF16)
        mean = jnp.concatenate(
            [mm(square[:, :256], mix[...]), mm(square[:, 256:], mix[...])], axis=1)
        query = (q * lax.rsqrt(mean + 1e-6) * scale_ref[...]).astype(BF16)
        queries[rows, :] = query
        key = head_norm_cols(mm_nt(wk_t[...], normed))
        value = mm(normed, wv_ref[...]).astype(BF16)
        set_heads(near_keys, near_values, key, value, BALL)
        for g in range(HEADS // GROUP):
            cols = slice(g * 256, (g + 1) * 256)
            qg = query[:, cols]
            for l in range(GROUP):
                p = jnp.exp2(mm(qg, near_keys[g, :, l * BALL:(l + 1) * BALL]))
                probs[:, l * BALL:(l + 1) * BALL] = p.astype(BF16)
                partial[:, l * 128:(l + 1) * 128] = (p[:, :128] + p[:, 128:]).astype(BF16)
            totals[rows, cols] = mm(probs[...], near_values[g])
            sums[rows, cols] = mm(partial[...], spread[...])
        return carry

    lax.fori_loop(0, NB, near, 0)
    own.wait()
    to_partner.wait()
    for copy in outs:
        copy.wait_send()
    for copy in onward:
        copy.wait()

    def far(ball, carry):
        rows = pl.ds(pl.multiple_of(ball * BALL, BALL), BALL)
        picked = []
        for j in range(OWNERS):
            picked.append(cand[chosen_ref[ball, j]])
        picked = jnp.concatenate(picked, axis=0)
        key = head_norm_cols(mm_nt(wpk_t[...], picked))
        value = mm(picked, wpv_ref[...]).astype(BF16)
        set_heads(far_keys, far_values, key, value, OWNERS * CK)
        attended = []
        for g in range(HEADS // GROUP):
            cols = slice(g * 256, (g + 1) * 256)
            qg = queries[rows, cols]
            for l in range(GROUP // 2):
                p = jnp.exp2(mm(qg, far_keys[g, :, l * 256:(l + 1) * 256]))
                partial[:, l * 256:(l + 1) * 256] = p.astype(BF16)
            total = totals[rows, cols] + mm(partial[...], far_values[g])
            denominator = sums[rows, cols] + mm(partial[...], spread[...])
            attended.append((total / denominator).astype(BF16))
        attended = jnp.concatenate(attended, axis=1)
        out_ref[rows, :] = (
            grouped_ref[rows, :].astype(F32) + mm(attended, wo_ref[...])).astype(BF16)
        return carry

    lax.fori_loop(0, NB, far, 0)


def attention(chosen, arrays):
    return pl.pallas_call(
        attention_kernel,
        in_specs=[pl.BlockSpec(memory_space=pltpu.SMEM)] + vmem(len(arrays)),
        out_specs=vmem(1)[0],
        out_shape=jax.ShapeDtypeStruct((ROWS, D), BF16),
        scratch_shapes=[
            pltpu.VMEM((10 * NB, CK, D), BF16),
            pltpu.VMEM((2, 256, GROUP * BALL), BF16),
            pltpu.VMEM((2, GROUP * BALL, 256), BF16),
            pltpu.VMEM((2, 256, GROUP * 128), BF16),
            pltpu.VMEM((2, GROUP * 128, 256), BF16),
            pltpu.VMEM((BALL, GROUP * BALL), BF16),
            pltpu.VMEM((BALL, GROUP * 128), BF16),
            pltpu.VMEM((ROWS, D), BF16),
            pltpu.VMEM((ROWS, D), F32),
            pltpu.VMEM((ROWS, D), F32),
            pltpu.VMEM((D, D), BF16),
            pltpu.VMEM((D, D), BF16),
            pltpu.VMEM((256, 256), BF16),
            pltpu.VMEM((GROUP * 128, 256), BF16),
            pltpu.SemaphoreType.DMA((9,)),
            pltpu.SemaphoreType.DMA((9,)),
            pltpu.SemaphoreType.DMA((1,)),
        ],
        compiler_params=pltpu.CompilerParams(
            collective_id=2, has_side_effects=True, vmem_limit_bytes=VMEM_LIMIT),
        name="attention",
    )(chosen, *arrays)


def finish_kernel(slot_ref, pos_ref, res_ref, wg_ref, wu_ref, wd_ref, gain_ref, out_ref,
                  col, ready, landed, send, recv, here):
    greet()

    def back(k):
        return pltpu.make_async_remote_copy(
            src_ref=ready.at[k], dst_ref=landed.at[k], send_sem=send.at[k],
            recv_sem=recv.at[k], device_id={"pts": behind(k)}, device_id_type=MESH)

    own = pltpu.make_async_copy(ready.at[0], landed.at[0], here.at[0])

    def prepare(c):
        hot = one_hot_cols(0, column(slot_ref[c]), ROWS)
        wide = mm(hot, res_ref[...])
        mean = jnp.mean(wide * wide, axis=-1, keepdims=True)
        ffn = (wide * lax.rsqrt(mean + 1e-5) * gain_ref[...]).astype(BF16)
        gate = mm(ffn, wg_ref[...])
        up = mm(ffn, wu_ref[...])
        hidden = (gate / (1.0 + jnp.exp(-gate)) * up).astype(BF16)
        result = (wide + mm(hidden, wd_ref[...])).astype(BF16)
        ready[pl.ds(pl.multiple_of(c * 8, 8), 8)] = result.reshape(8, EACH, D)

    prepare(0)
    met()

    def more(c):
        prepare(c)
        first = c * 8 - 8
        steps(jnp.maximum(first, 1), first + 8, lambda k: back(k).start())

    steps(1, NB, more)
    own.start()
    steps(PEERS - 8, PEERS, lambda k: back(k).start())
    col[...] = column(pos_ref[...])
    own.wait()

    def place(c, first):
        steps(1 if first else c * 8, c * 8 + 8, lambda k: back(k).wait_recv())
        chunk = landed[pl.ds(pl.multiple_of(c * 8, 8), 8)].reshape(256, D)
        for b in range(NB):
            at = slice(b * 256, (b + 1) * 256)
            part = mm(one_hot_cols(c * 256, col[at, :], 256), chunk).astype(BF16)
            if first:
                out_ref[at, :] = part
            else:
                out_ref[at, :] = out_ref[at, :] + part

    place(0, True)
    steps(1, NB, lambda c: place(c, False))
    steps(1, PEERS, lambda k: back(k).wait_send())


def finish(*arrays):
    return pl.pallas_call(
        finish_kernel,
        in_specs=vmem(len(arrays)),
        out_specs=vmem(1)[0],
        out_shape=jax.ShapeDtypeStruct((ROWS, D), BF16),
        scratch_shapes=[
            pltpu.VMEM((ROWS, 1), jnp.int32),
            pltpu.VMEM((PEERS, EACH, D), BF16),
            pltpu.VMEM((PEERS, EACH, D), BF16),
            pltpu.SemaphoreType.DMA((PEERS,)),
            pltpu.SemaphoreType.DMA((PEERS,)),
            pltpu.SemaphoreType.DMA((1,)),
        ],
        compiler_params=pltpu.CompilerParams(
            collective_id=1, has_side_effects=True, vmem_limit_bytes=VMEM_LIMIT),
        name="finish",
    )(*arrays)


def on_device(
    points, point_row_index, neighbour_ball_list, attention_norm_gain, query_weight,
    key_weight, value_weight, pooled_key_weight, pooled_value_weight, head_score_scale,
    output_weight, feedforward_norm_gain, gate_weight, up_weight, down_weight,
):
    me = lax.axis_index("pts")
    grouped, normed, pooled, pos, slot = front(
        point_row_index.reshape(1, ROWS), points, attention_norm_gain.reshape(1, D))
    owner = neighbour_ball_list // NB
    place_of = jnp.mod(owner // 2 - me // 2 + 2, CHIPS) * 2 + owner % 2
    chosen = place_of * NB + neighbour_ball_list % NB
    scale = jnp.repeat(head_score_scale * (math.log2(math.e) / HD), HD).reshape(1, D)
    residual = attention(
        chosen,
        (normed, grouped, pooled, query_weight, key_weight, value_weight, pooled_key_weight,
         pooled_value_weight, output_weight, scale))
    return finish(slot, pos, residual, gate_weight, up_weight, down_weight,
                  feedforward_norm_gain.reshape(1, D))


def solution(mesh):
    return jax.shard_map(
        on_device,
        mesh=mesh,
        in_specs=(
            P(("rep", "pts"), None), P(("rep", "pts")), P(("rep", "pts"), None),
            P(), P(), P(), P(), P(), P(), P(), P(), P(), P(), P(), P(),
        ),
        out_specs=P(("rep", "pts"), None),
        check_vma=False,
    )
```

```python
import functools
import math

import jax
import jax.numpy as jnp
from jax import lax
from jax.experimental import pallas as pl
from jax.experimental.pallas import tpu as pltpu
from jax.sharding import PartitionSpec as P

BALL = 256
POOL = 8
OWNERS = 4
D = 512
HEADS = 16
HD = 32
FF = 1024
ROWS = 2048
PEERS = 64
EACH = 32
CK = BALL // POOL
NB = ROWS // BALL
STRIDE = 13
LAG = 16
INVERSE = 5
CHIPS = PEERS // 2
MESH = pl.DeviceIdType.MESH
F32 = jnp.float32
BF16 = jnp.bfloat16
VMEM_LIMIT = 56 * 1024 * 1024


def vmem(n):
    return [pl.BlockSpec(memory_space=pltpu.VMEM)] * n


def mm(a, b):
    return jnp.dot(a, b, preferred_element_type=F32)


def mm_nt(a, b):
    return lax.dot_general(a, b, (((1,), (1,)), ((), ())), preferred_element_type=F32)


def one_hot_rows(start, count, row):
    ids = lax.broadcasted_iota(jnp.int32, (count, row.shape[1]), 0) + start
    return jnp.where(ids == row, 1.0, 0.0).astype(BF16)


def one_hot_cols(start, col, width):
    ids = lax.broadcasted_iota(jnp.int32, (col.shape[0], width), 1) + start
    return jnp.where(ids == col, 1.0, 0.0).astype(BF16)


def column(row):
    wide = jnp.broadcast_to(row.astype(F32), (8, row.shape[1]))
    return wide.T[:, :1].astype(jnp.int32)


def ahead(k):
    return (lax.axis_index("pts") + STRIDE * k) % PEERS


def behind(k):
    return (lax.axis_index("pts") + PEERS * STRIDE - STRIDE * k) % PEERS


def greet():
    barrier = pltpu.get_barrier_semaphore()

    def signal(k, carry):
        pl.semaphore_signal(barrier, inc=1, device_id={"pts": ahead(k)}, device_id_type=MESH)
        return carry

    lax.fori_loop(1, PEERS, signal, 0)


def met():
    pl.semaphore_wait(pltpu.get_barrier_semaphore(), PEERS - 1)


def steps(lo, hi, body):
    def step(k, carry):
        body(k)
        return carry

    lax.fori_loop(lo, hi, step, 0)


def front_kernel(
    row_ref, x_ref, gain_ref, grouped_ref, normed_ref, pooled_ref, pos_ref, slot_ref,
    col, ready, numbers, landed, landed_numbers, send, recv, nsend, nrecv, here,
):
    me = lax.axis_index("pts")
    greet()
    row = row_ref[...]
    col[...] = column(row)

    def count(j, acc):
        part = col[pl.ds(pl.multiple_of(j * 256, 256), 256), :]
        less = jnp.where(part < row, 1.0, 0.0)
        return acc + jnp.sum(less.reshape(32, 8, ROWS), axis=0)

    acc = lax.fori_loop(0, NB, count, jnp.zeros((8, ROWS), F32))
    rank = jnp.sum(acc, axis=0, keepdims=True).astype(jnp.int32)
    turn = (((rank >> 5) + PEERS - me) * INVERSE) & (PEERS - 1)
    pos_ref[...] = turn * EACH + (rank & (EACH - 1))
    slot = row & (ROWS - 1)
    parts = jnp.concatenate(
        [(slot >> 6).astype(F32), (slot & 63).astype(F32), jnp.zeros((6, ROWS), F32)],
        axis=0).astype(BF16)

    def rows(k):
        return pltpu.make_async_remote_copy(
            src_ref=ready.at[k], dst_ref=landed.at[k], send_sem=send.at[k],
            recv_sem=recv.at[k], device_id={"pts": ahead(k)}, device_id_type=MESH)

    def ids(k):
        return pltpu.make_async_remote_copy(
            src_ref=numbers.at[k // 4], dst_ref=landed_numbers.at[k], send_sem=nsend.at[k],
            recv_sem=nrecv.at[k], device_id={"pts": ahead(k)}, device_id_type=MESH)

    def start(k):
        ids(k).start()
        rows(k).start()

    def prepare(c):
        hot = one_hot_rows(c * 256, 256, pos_ref[...])
        ready[pl.ds(pl.multiple_of(c * 8, 8), 8)] = mm(hot, x_ref[...]).astype(BF16).reshape(
            8, EACH, D)
        back = mm_nt(parts, hot)
        whole = (back[0:1] * 64.0 + back[1:2]).astype(jnp.int32)
        numbers[2 * c] = whole[:, :128]
        numbers[2 * c + 1] = whole[:, 128:]

    prepare(0)
    met()
    own = pltpu.make_async_copy(ready.at[0], landed.at[0], here.at[0])
    own_ids = pltpu.make_async_copy(numbers.at[0], landed_numbers.at[0], here.at[1])

    def more(c):
        prepare(c)
        first = c * 8 - 8
        steps(jnp.maximum(first, 1), first + 8, start)

    steps(1, NB, more)
    own.start()
    own_ids.start()
    steps(PEERS - 8, PEERS, start)
    own.wait()
    own_ids.wait()

    def place(c, first):
        def arrive(k):
            ids(k).wait_recv()
            rows(k).wait_recv()

        steps(1 if first else c * 8, c * 8 + 8, arrive)
        got = landed_numbers[pl.ds(pl.multiple_of(c * 8, 8), 8)]
        lane = lax.broadcasted_iota(jnp.int32, got.shape, 2) // EACH
        turn = lax.broadcasted_iota(jnp.int32, got.shape, 0) & 3
        got = jnp.where(lane == turn, got, 0)
        halves = [got[0] + got[1] + got[2] + got[3], got[4] + got[5] + got[6] + got[7]]
        number = jnp.concatenate(halves, axis=1)
        slot_ref[c] = number
        chunk = landed[pl.ds(pl.multiple_of(c * 8, 8), 8)].reshape(256, D)
        for b in range(NB):
            at = slice(b * BALL, (b + 1) * BALL)
            part = mm(one_hot_rows(b * BALL, BALL, number), chunk).astype(BF16)
            if first:
                grouped_ref[at, :] = part
            else:
                grouped_ref[at, :] = grouped_ref[at, :] + part

    place(0, True)
    steps(1, NB, lambda c: place(c, False))

    r = lax.broadcasted_iota(jnp.int32, (CK, BALL), 0)
    c = lax.broadcasted_iota(jnp.int32, (CK, BALL), 1)
    pool = jnp.where(c // POOL == r, 1.0 / POOL, 0.0).astype(BF16)

    def norm(b):
        at = pl.ds(pl.multiple_of(b * BALL, BALL), BALL)
        wide = grouped_ref[at, :].astype(F32)
        mean = jnp.mean(wide * wide, axis=-1, keepdims=True)
        normed = (wide * lax.rsqrt(mean + 1e-5) * gain_ref[...]).astype(BF16)
        normed_ref[at, :] = normed
        pooled_ref[b] = mm(pool, normed).astype(BF16)

    steps(0, NB, norm)

    def sent(k):
        ids(k).wait_send()
        rows(k).wait_send()

    steps(1, PEERS, sent)


def front(row, x, gain):
    return pl.pallas_call(
        front_kernel,
        in_specs=vmem(3),
        out_specs=vmem(5),
        out_shape=[
            jax.ShapeDtypeStruct((ROWS, D), BF16),
            jax.ShapeDtypeStruct((ROWS, D), BF16),
            jax.ShapeDtypeStruct((NB, CK, D), BF16),
            jax.ShapeDtypeStruct((1, ROWS), jnp.int32),
            jax.ShapeDtypeStruct((NB, 1, 256), jnp.int32),
        ],
        scratch_shapes=[
            pltpu.VMEM((ROWS, 1), jnp.int32),
            pltpu.VMEM((PEERS, EACH, D), BF16),
            pltpu.VMEM((16, 1, 128), jnp.int32),
            pltpu.VMEM((PEERS, EACH, D), BF16),
            pltpu.VMEM((PEERS, 1, 128), jnp.int32),
            pltpu.SemaphoreType.DMA((PEERS,)),
            pltpu.SemaphoreType.DMA((PEERS,)),
            pltpu.SemaphoreType.DMA((PEERS,)),
            pltpu.SemaphoreType.DMA((PEERS,)),
            pltpu.SemaphoreType.DMA((2,)),
        ],
        compiler_params=pltpu.CompilerParams(
            collective_id=0, has_side_effects=True, vmem_limit_bytes=VMEM_LIMIT),
        name="front",
    )(row, x, gain)


def head_norm_rows(u, mix):
    square = (u * u).astype(BF16)
    mean = jnp.concatenate([mm(square[:, :256], mix), mm(square[:, 256:], mix)], axis=1)
    return (u * lax.rsqrt(mean + 1e-6)).astype(BF16)


def block_ones(rows, per_row, per_col, value):
    a = lax.broadcasted_iota(jnp.int32, (rows, 256), 0) // per_row
    b = lax.broadcasted_iota(jnp.int32, (rows, 256), 1) // per_col
    return jnp.where(a == b, value, 0.0).astype(BF16)


def set_queries(spread, query):
    for h in range(HEADS):
        at = (h % 4) * HD
        spread[h, at:at + HD, :] = query[h]


def head_sums(key, value, spread, probs, finish_head):
    ones = jnp.ones((16, value.shape[1]), BF16)
    count = value.shape[1]

    def scores(h):
        group = slice((h // 4) * 128, (h // 4) * 128 + 128)
        probs[h % LAG, :count, :] = jnp.exp2(mm(key[:, group], spread[h])).astype(BF16)

    def weigh(h):
        rows = jnp.concatenate([value[h * HD:(h + 1) * HD, :], ones], axis=0)
        finish_head(h, mm(rows, probs[h % LAG, :count, :])[:HD + 8])

    for h in range(HEADS + LAG - 1):
        if h < HEADS:
            scores(h)
        if h >= LAG - 1:
            weigh(h - LAG + 1)


def attention_kernel(
    chosen_ref, scale_ref, normed_ref, grouped_ref, pooled_ref, wq_ref, wk_ref, wv_ref,
    wpk_ref, wpv_ref, wo_ref, out_ref,
    cand, spread, queries, totals, probs, turned, wqv_t, wpv_t, mix, send, recv, here,
):
    me = lax.axis_index("pts")
    core = me % 2
    chip = me // 2
    partner = chip * 2 + 1 - core
    def chip_at(e):
        return ((chip + e + CHIPS) % CHIPS) * 2 + core

    barrier = pltpu.get_barrier_semaphore()
    for d in (partner, chip_at(1), chip_at(-1)):
        pl.semaphore_signal(barrier, inc=1, device_id={"pts": d}, device_id_type=MESH)
    pl.semaphore_wait(barrier, 3)

    def block(slot):
        return cand.at[pl.ds(slot * NB, NB)]

    def remote(src, slot, at, d):
        return pltpu.make_async_remote_copy(
            src_ref=src, dst_ref=block(slot), send_sem=send.at[at], recv_sem=recv.at[at],
            device_id={"pts": d}, device_id_type=MESH)

    def slot(e):
        return (2 - e) * 2 + core

    outs = [remote(pooled_ref, slot(e), 1 + i, chip_at(e)) for i, e in enumerate((1, -1))]
    for copy in outs:
        copy.start()
    to_partner = remote(pooled_ref, slot(0), 0, partner)
    to_partner.start()
    own = pltpu.make_async_copy(pooled_ref, block(slot(0)), here.at[0])
    own.start()
    farther = [remote(block(slot(e)), slot(2 * e), 3 + i, chip_at(e))
               for i, e in enumerate((1, -1))]
    onward = [remote(block(slot(e)), slot(e), 5 + i, partner)
              for i, e in enumerate((1, -1, 2, -2))]

    spread[...] = jnp.zeros_like(spread)
    wqv_t[:D, :] = wq_ref[...].T
    wqv_t[D:, :] = wv_ref[...].T
    wpv_t[...] = wpv_ref[...].T
    mix[...] = block_ones(256, HD, HD, 1.0 / HD)

    def near(ball, carry):
        @pl.when(ball == 4)
        def _():
            for i in range(2):
                outs[i].wait_recv()
                farther[i].start()
                onward[i].start()

        @pl.when(ball == 7)
        def _():
            for i in range(2):
                farther[i].wait_recv()
                onward[2 + i].start()

        rows = pl.ds(pl.multiple_of(ball * BALL, BALL), BALL)
        normed = normed_ref[rows, :]
        both = mm_nt(wqv_t[...], normed)
        shaped = both[:D].reshape(HEADS, HD, BALL)
        mean = jnp.mean(shaped * shaped, axis=1, keepdims=True)
        factor = lax.rsqrt(mean + 1e-6)
        for h in range(HEADS):
            queries[ball, h] = (shaped[h] * (factor[h] * (scale_ref[h] * (math.log2(math.e) / HD)))).astype(BF16)
        value = both[D:].astype(BF16)
        key = head_norm_rows(mm(normed, wk_ref[...]), mix[...])
        set_queries(spread, queries.at[ball])

        def keep(h, total):
            totals[ball, h] = total

        head_sums(key, value, spread, probs, keep)
        return carry

    lax.fori_loop(0, NB, near, 0)
    own.wait()
    to_partner.wait()
    for copy in outs + farther:
        copy.wait_send()
    for copy in onward:
        copy.wait()

    def far(ball, carry):
        rows = pl.ds(pl.multiple_of(ball * BALL, BALL), BALL)
        picked = []
        for j in range(OWNERS):
            picked.append(cand[chosen_ref[ball, j]])
        picked = jnp.concatenate(picked, axis=0)
        key = head_norm_rows(mm(picked, wpk_ref[...]), mix[...])
        value = mm_nt(wpv_t[...], picked).astype(BF16)
        set_queries(spread, queries.at[ball])

        def close(h, total):
            total = totals[ball, h] + total
            turned[h * HD:(h + 1) * HD, :] = (total[:HD] / total[HD:HD + 1]).astype(BF16)

        head_sums(key, value, spread, probs, close)
        attended = turned[...].T
        out_ref[rows, :] = (
            grouped_ref[rows, :].astype(F32) + mm(attended, wo_ref[...])).astype(BF16)
        return carry

    lax.fori_loop(0, NB, far, 0)


def attention(chosen, scale, arrays):
    return pl.pallas_call(
        attention_kernel,
        in_specs=[pl.BlockSpec(memory_space=pltpu.SMEM)] * 2 + vmem(len(arrays)),
        out_specs=vmem(1)[0],
        out_shape=jax.ShapeDtypeStruct((ROWS, D), BF16),
        scratch_shapes=[
            pltpu.VMEM((10 * NB, CK, D), BF16),
            pltpu.VMEM((HEADS, 128, BALL), BF16),
            pltpu.VMEM((NB, HEADS, HD, BALL), BF16),
            pltpu.VMEM((NB, HEADS, HD + 8, BALL), F32),
            pltpu.VMEM((LAG, BALL, BALL), BF16),
            pltpu.VMEM((D, BALL), BF16),
            pltpu.VMEM((2 * D, D), BF16),
            pltpu.VMEM((D, D), BF16),
            pltpu.VMEM((256, 256), BF16),
            pltpu.SemaphoreType.DMA((9,)),
            pltpu.SemaphoreType.DMA((9,)),
            pltpu.SemaphoreType.DMA((1,)),
        ],
        compiler_params=pltpu.CompilerParams(
            collective_id=2, has_side_effects=True, vmem_limit_bytes=VMEM_LIMIT),
        name="attention",
    )(chosen, scale, *arrays)


def finish_kernel(slot_ref, pos_ref, res_ref, wg_ref, wu_ref, wd_ref, gain_ref, out_ref,
                  col, ready, landed, send, recv, here):
    greet()

    def back(k):
        return pltpu.make_async_remote_copy(
            src_ref=ready.at[k], dst_ref=landed.at[k], send_sem=send.at[k],
            recv_sem=recv.at[k], device_id={"pts": behind(k)}, device_id_type=MESH)

    own = pltpu.make_async_copy(ready.at[0], landed.at[0], here.at[0])

    def prepare(c, between=None):
        hot = one_hot_cols(0, column(slot_ref[c]), ROWS)
        wide = mm(hot, res_ref[...])
        if between is not None:
            between()
        mean = jnp.mean(wide * wide, axis=-1, keepdims=True)
        ffn = (wide * lax.rsqrt(mean + 1e-5) * gain_ref[...]).astype(BF16)
        gate = mm(ffn, wg_ref[...])
        up = mm(ffn, wu_ref[...])
        hidden = (gate / (1.0 + jnp.exp(-gate)) * up).astype(BF16)
        result = (wide + mm(hidden, wd_ref[...])).astype(BF16)
        ready[pl.ds(pl.multiple_of(c * 8, 8), 8)] = result.reshape(8, EACH, D)

    prepare(0)
    met()

    def more(c):
        first = c * 8 - 8
        prepare(c, lambda: steps(
            jnp.maximum(first, 1), first + 8, lambda k: back(k).start()))

    steps(1, NB, more)
    own.start()
    steps(PEERS - 8, PEERS, lambda k: back(k).start())
    col[...] = column(pos_ref[...])
    own.wait()

    def place(c, store):
        chunk = landed[pl.ds(pl.multiple_of(c * 8, 8), 8)].reshape(256, D)
        for b in range(NB):
            at = slice(b * 256, (b + 1) * 256)
            store(at, mm(one_hot_cols(c * 256, col[at, :], 256), chunk).astype(BF16))

    def arrive(lo, hi):
        steps(lo, hi, lambda k: back(k).wait_recv())

    def set_out(at, part):
        out_ref[at, :] = part

    def add(at, part):
        out_ref[at, :] = out_ref[at, :] + part

    def middle(c):
        arrive(c * 8, c * 8 + 8)
        place(c, add)

    arrive(1, 8)
    place(0, set_out)
    steps(1, NB, middle)
    steps(1, PEERS, lambda k: back(k).wait_send())


def finish(*arrays):
    return pl.pallas_call(
        finish_kernel,
        in_specs=vmem(len(arrays)),
        out_specs=vmem(1)[0],
        out_shape=jax.ShapeDtypeStruct((ROWS, D), BF16),
        scratch_shapes=[
            pltpu.VMEM((ROWS, 1), jnp.int32),
            pltpu.VMEM((PEERS, EACH, D), BF16),
            pltpu.VMEM((PEERS, EACH, D), BF16),
            pltpu.SemaphoreType.DMA((PEERS,)),
            pltpu.SemaphoreType.DMA((PEERS,)),
            pltpu.SemaphoreType.DMA((1,)),
        ],
        compiler_params=pltpu.CompilerParams(
            collective_id=1, has_side_effects=True, vmem_limit_bytes=VMEM_LIMIT),
        name="finish",
    )(*arrays)


def on_device(
    points, point_row_index, neighbour_ball_list, attention_norm_gain, query_weight,
    key_weight, value_weight, pooled_key_weight, pooled_value_weight, head_score_scale,
    output_weight, feedforward_norm_gain, gate_weight, up_weight, down_weight,
):
    me = lax.axis_index("pts")
    grouped, normed, pooled, pos, slot = front(
        point_row_index.reshape(1, ROWS), points, attention_norm_gain.reshape(1, D))
    owner = neighbour_ball_list // NB
    place_of = jnp.mod(owner // 2 - me // 2 + 2, CHIPS) * 2 + owner % 2
    chosen = place_of * NB + neighbour_ball_list % NB
    residual = attention(
        chosen, head_score_scale,
        (normed, grouped, pooled, query_weight, key_weight, value_weight, pooled_key_weight,
         pooled_value_weight, output_weight))
    return finish(slot, pos, residual, gate_weight, up_weight, down_weight,
                  feedforward_norm_gain.reshape(1, D))


def solution(mesh):
    return jax.shard_map(
        on_device,
        mesh=mesh,
        in_specs=(
            P(("rep", "pts"), None), P(("rep", "pts")), P(("rep", "pts"), None),
            P(), P(), P(), P(), P(), P(), P(), P(), P(), P(), P(), P(),
        ),
        out_specs=P(("rep", "pts"), None),
        check_vma=False,
    )
```

```python
import functools
import math

import jax
import jax.numpy as jnp
from jax import lax
from jax.experimental import pallas as pl
from jax.experimental.pallas import tpu as pltpu
from jax.sharding import PartitionSpec as P

BALL = 256
POOL = 8
OWNERS = 4
D = 512
HEADS = 16
HD = 32
FF = 1024
ROWS = 2048
PEERS = 64
EACH = 32
CK = BALL // POOL
NB = ROWS // BALL
STRIDE = 37
LAG = 16
INVERSE = 45
CHIPS = PEERS // 2
MESH = pl.DeviceIdType.MESH
F32 = jnp.float32
BF16 = jnp.bfloat16
VMEM_LIMIT = 56 * 1024 * 1024


def vmem(n):
    return [pl.BlockSpec(memory_space=pltpu.VMEM)] * n


def mm(a, b):
    return jnp.dot(a, b, preferred_element_type=F32)


def mm_nt(a, b):
    return lax.dot_general(a, b, (((1,), (1,)), ((), ())), preferred_element_type=F32)


def one_hot_rows(start, count, row):
    ids = lax.broadcasted_iota(jnp.int32, (count, row.shape[1]), 0) + start
    return jnp.where(ids == row, 1.0, 0.0).astype(BF16)


def one_hot_cols(start, col, width):
    ids = lax.broadcasted_iota(jnp.int32, (col.shape[0], width), 1) + start
    return jnp.where(ids == col, 1.0, 0.0).astype(BF16)


def column(row):
    wide = jnp.broadcast_to(row.astype(F32), (8, row.shape[1]))
    return wide.T[:, :1].astype(jnp.int32)


def ahead(k):
    return (lax.axis_index("pts") + STRIDE * k) % PEERS


def behind(k):
    return (lax.axis_index("pts") + PEERS * STRIDE - STRIDE * k) % PEERS


def greet():
    barrier = pltpu.get_barrier_semaphore()

    def signal(k, carry):
        pl.semaphore_signal(barrier, inc=1, device_id={"pts": ahead(k)}, device_id_type=MESH)
        return carry

    lax.fori_loop(1, PEERS, signal, 0)


def met():
    pl.semaphore_wait(pltpu.get_barrier_semaphore(), PEERS - 1)


def steps(lo, hi, body):
    def step(k, carry):
        body(k)
        return carry

    lax.fori_loop(lo, hi, step, 0)


def front_kernel(
    row_ref, x_ref, gain_ref, grouped_ref, normed_ref, pooled_ref, pos_ref, slot_ref,
    col, ready, numbers, landed, landed_numbers, send, recv, nsend, nrecv, here,
):
    me = lax.axis_index("pts")
    greet()
    row = row_ref[...]
    col[...] = column(row)

    def count(j, acc):
        part = col[pl.ds(pl.multiple_of(j * 256, 256), 256), :]
        less = jnp.where(part < row, 1.0, 0.0)
        return acc + jnp.sum(less.reshape(32, 8, ROWS), axis=0)

    acc = lax.fori_loop(0, NB, count, jnp.zeros((8, ROWS), F32))
    rank = jnp.sum(acc, axis=0, keepdims=True).astype(jnp.int32)
    turn = (((rank >> 5) + PEERS - me) * INVERSE) & (PEERS - 1)
    pos_ref[...] = turn * EACH + (rank & (EACH - 1))
    slot = row & (ROWS - 1)
    parts = jnp.concatenate(
        [(slot >> 6).astype(F32), (slot & 63).astype(F32), jnp.zeros((6, ROWS), F32)],
        axis=0).astype(BF16)

    def rows(k):
        return pltpu.make_async_remote_copy(
            src_ref=ready.at[k], dst_ref=landed.at[k], send_sem=send.at[k],
            recv_sem=recv.at[k], device_id={"pts": ahead(k)}, device_id_type=MESH)

    def ids(k):
        return pltpu.make_async_remote_copy(
            src_ref=numbers.at[k // 4], dst_ref=landed_numbers.at[k], send_sem=nsend.at[k],
            recv_sem=nrecv.at[k], device_id={"pts": ahead(k)}, device_id_type=MESH)

    def start(k):
        ids(k).start()
        rows(k).start()

    def prepare(c):
        hot = one_hot_rows(c * 256, 256, pos_ref[...])
        ready[pl.ds(pl.multiple_of(c * 8, 8), 8)] = mm(hot, x_ref[...]).astype(BF16).reshape(
            8, EACH, D)
        back = mm_nt(parts, hot)
        whole = (back[0:1] * 64.0 + back[1:2]).astype(jnp.int32)
        numbers[2 * c] = whole[:, :128]
        numbers[2 * c + 1] = whole[:, 128:]

    prepare(0)
    met()
    own = pltpu.make_async_copy(ready.at[0], landed.at[0], here.at[0])
    own_ids = pltpu.make_async_copy(numbers.at[0], landed_numbers.at[0], here.at[1])

    def more(c):
        prepare(c)
        first = c * 8 - 8
        steps(jnp.maximum(first, 1), first + 8, start)

    steps(1, NB, more)
    own.start()
    own_ids.start()
    steps(PEERS - 8, PEERS, start)
    own.wait()
    own_ids.wait()

    def place(c, first):
        def arrive(k):
            ids(k).wait_recv()
            rows(k).wait_recv()

        steps(1 if first else c * 8, c * 8 + 8, arrive)
        got = landed_numbers[pl.ds(pl.multiple_of(c * 8, 8), 8)]
        lane = lax.broadcasted_iota(jnp.int32, got.shape, 2) // EACH
        turn = lax.broadcasted_iota(jnp.int32, got.shape, 0) & 3
        got = jnp.where(lane == turn, got, 0)
        halves = [got[0] + got[1] + got[2] + got[3], got[4] + got[5] + got[6] + got[7]]
        number = jnp.concatenate(halves, axis=1)
        slot_ref[c] = number
        chunk = landed[pl.ds(pl.multiple_of(c * 8, 8), 8)].reshape(256, D)
        for b in range(NB):
            at = slice(b * BALL, (b + 1) * BALL)
            part = mm(one_hot_rows(b * BALL, BALL, number), chunk).astype(BF16)
            if first:
                grouped_ref[at, :] = part
            else:
                grouped_ref[at, :] = grouped_ref[at, :] + part

    place(0, True)
    steps(1, NB, lambda c: place(c, False))

    r = lax.broadcasted_iota(jnp.int32, (CK, BALL), 0)
    c = lax.broadcasted_iota(jnp.int32, (CK, BALL), 1)
    pool = jnp.where(c // POOL == r, 1.0 / POOL, 0.0).astype(BF16)

    def norm(b):
        at = pl.ds(pl.multiple_of(b * BALL, BALL), BALL)
        wide = grouped_ref[at, :].astype(F32)
        mean = jnp.mean(wide * wide, axis=-1, keepdims=True)
        normed = (wide * lax.rsqrt(mean + 1e-5) * gain_ref[...]).astype(BF16)
        normed_ref[at, :] = normed
        pooled_ref[b] = mm(pool, normed).astype(BF16)

    steps(0, NB, norm)

    def sent(k):
        ids(k).wait_send()
        rows(k).wait_send()

    steps(1, PEERS, sent)


def front(row, x, gain):
    return pl.pallas_call(
        front_kernel,
        in_specs=vmem(3),
        out_specs=vmem(5),
        out_shape=[
            jax.ShapeDtypeStruct((ROWS, D), BF16),
            jax.ShapeDtypeStruct((ROWS, D), BF16),
            jax.ShapeDtypeStruct((NB, CK, D), BF16),
            jax.ShapeDtypeStruct((1, ROWS), jnp.int32),
            jax.ShapeDtypeStruct((NB, 1, 256), jnp.int32),
        ],
        scratch_shapes=[
            pltpu.VMEM((ROWS, 1), jnp.int32),
            pltpu.VMEM((PEERS, EACH, D), BF16),
            pltpu.VMEM((16, 1, 128), jnp.int32),
            pltpu.VMEM((PEERS, EACH, D), BF16),
            pltpu.VMEM((PEERS, 1, 128), jnp.int32),
            pltpu.SemaphoreType.DMA((PEERS,)),
            pltpu.SemaphoreType.DMA((PEERS,)),
            pltpu.SemaphoreType.DMA((PEERS,)),
            pltpu.SemaphoreType.DMA((PEERS,)),
            pltpu.SemaphoreType.DMA((2,)),
        ],
        compiler_params=pltpu.CompilerParams(
            collective_id=0, has_side_effects=True, vmem_limit_bytes=VMEM_LIMIT),
        name="front",
    )(row, x, gain)


def head_norm_rows(u, mix):
    square = (u * u).astype(BF16)
    mean = jnp.concatenate([mm(square[:, :256], mix), mm(square[:, 256:], mix)], axis=1)
    return (u * lax.rsqrt(mean + 1e-6)).astype(BF16)


def block_ones(rows, per_row, per_col, value):
    a = lax.broadcasted_iota(jnp.int32, (rows, 256), 0) // per_row
    b = lax.broadcasted_iota(jnp.int32, (rows, 256), 1) // per_col
    return jnp.where(a == b, value, 0.0).astype(BF16)


def set_queries(spread, query):
    for h in range(HEADS):
        at = (h % 4) * HD
        spread[h, at:at + HD, :] = query[h]


def head_sums(key, value, spread, probs, finish_head):
    ones = jnp.ones((16, value.shape[1]), BF16)
    count = value.shape[1]

    def scores(h):
        group = slice((h // 4) * 128, (h // 4) * 128 + 128)
        probs[h % LAG, :count, :] = jnp.exp2(mm(key[:, group], spread[h])).astype(BF16)

    def weigh(h):
        rows = jnp.concatenate([value[h * HD:(h + 1) * HD, :], ones], axis=0)
        finish_head(h, mm(rows, probs[h % LAG, :count, :])[:HD + 8])

    for h in range(HEADS + LAG - 1):
        if h < HEADS:
            scores(h)
        if h >= LAG - 1:
            weigh(h - LAG + 1)


def attention_kernel(
    chosen_ref, scale_ref, normed_ref, grouped_ref, pooled_ref, wq_ref, wk_ref, wv_ref,
    wpk_ref, wpv_ref, wo_ref, out_ref,
    cand, spread, queries, totals, probs, turned, wqv_t, wpv_t, mix, send, recv, here,
):
    me = lax.axis_index("pts")
    core = me % 2
    chip = me // 2
    partner = chip * 2 + 1 - core
    def chip_at(e):
        return ((chip + e + CHIPS) % CHIPS) * 2 + core

    barrier = pltpu.get_barrier_semaphore()
    for d in (partner, chip_at(1), chip_at(-1)):
        pl.semaphore_signal(barrier, inc=1, device_id={"pts": d}, device_id_type=MESH)
    pl.semaphore_wait(barrier, 3)

    half = NB // 2

    def slot(e):
        return (2 - e) * 2 + core

    def part(at, h):
        return cand.at[pl.ds(at * NB + h * half, half)]

    def remote(src, at, h, sem, d):
        return pltpu.make_async_remote_copy(
            src_ref=src, dst_ref=part(at, h), send_sem=send.at[sem], recv_sem=recv.at[sem],
            device_id={"pts": d}, device_id_type=MESH)

    def mine(h):
        return pooled_ref.at[pl.ds(h * half, half)]

    sides = (1, -1)
    outs = [[remote(mine(h), slot(e), h, h * 2 + i, chip_at(e)) for i, e in enumerate(sides)]
            for h in range(2)]
    farther = [[remote(part(slot(e), h), slot(2 * e), h, 4 + h * 2 + i, chip_at(e))
                for i, e in enumerate(sides)] for h in range(2)]
    onward = [[remote(part(slot(e), h), slot(e), h, 8 + h * 4 + i, partner)
               for i, e in enumerate((1, -1, 2, -2))] for h in range(2)]
    to_partner = [remote(mine(h), slot(0), h, 16 + h, partner) for h in range(2)]
    for copy in outs[0] + outs[1] + to_partner:
        copy.start()
    own = pltpu.make_async_copy(pooled_ref, cand.at[pl.ds(slot(0) * NB, NB)], here.at[0])
    own.start()

    spread[...] = jnp.zeros_like(spread)
    wqv_t[:D, :] = wq_ref[...].T
    wqv_t[D:, :] = wv_ref[...].T
    wpv_t[...] = wpv_ref[...].T
    mix[...] = block_ones(256, HD, HD, 1.0 / HD)

    def near(ball, carry):
        for h, at in enumerate((3, 4)):
            @pl.when(ball == at)
            def _():
                for i in range(2):
                    outs[h][i].wait_recv()
                    farther[h][i].start()
                    onward[h][i].start()

        for h, at in enumerate((6, 7)):
            @pl.when(ball == at)
            def _():
                for i in range(2):
                    farther[h][i].wait_recv()
                    onward[h][2 + i].start()

        rows = pl.ds(pl.multiple_of(ball * BALL, BALL), BALL)
        normed = normed_ref[rows, :]
        both = mm_nt(wqv_t[...], normed)
        shaped = both[:D].reshape(HEADS, HD, BALL)
        mean = jnp.mean(shaped * shaped, axis=1, keepdims=True)
        factor = lax.rsqrt(mean + 1e-6)
        for h in range(HEADS):
            queries[ball, h] = (shaped[h] * (factor[h] * (scale_ref[h] * (math.log2(math.e) / HD)))).astype(BF16)
        value = both[D:].astype(BF16)
        key = head_norm_rows(mm(normed, wk_ref[...]), mix[...])
        set_queries(spread, queries.at[ball])

        def keep(h, total):
            totals[ball, h] = total

        head_sums(key, value, spread, probs, keep)
        return carry

    lax.fori_loop(0, NB, near, 0)
    own.wait()
    for h in range(2):
        to_partner[h].wait()
        for copy in outs[h] + farther[h]:
            copy.wait_send()
        for copy in onward[h]:
            copy.wait()

    def far(ball, carry):
        rows = pl.ds(pl.multiple_of(ball * BALL, BALL), BALL)
        picked = []
        for j in range(OWNERS):
            picked.append(cand[chosen_ref[ball, j]])
        picked = jnp.concatenate(picked, axis=0)
        key = head_norm_rows(mm(picked, wpk_ref[...]), mix[...])
        value = mm_nt(wpv_t[...], picked).astype(BF16)
        set_queries(spread, queries.at[ball])

        def close(h, total):
            total = totals[ball, h] + total
            turned[h * HD:(h + 1) * HD, :] = (total[:HD] / total[HD:HD + 1]).astype(BF16)

        head_sums(key, value, spread, probs, close)
        attended = turned[...].T
        out_ref[rows, :] = (
            grouped_ref[rows, :].astype(F32) + mm(attended, wo_ref[...])).astype(BF16)
        return carry

    lax.fori_loop(0, NB, far, 0)


def attention(chosen, scale, arrays):
    return pl.pallas_call(
        attention_kernel,
        in_specs=[pl.BlockSpec(memory_space=pltpu.SMEM)] * 2 + vmem(len(arrays)),
        out_specs=vmem(1)[0],
        out_shape=jax.ShapeDtypeStruct((ROWS, D), BF16),
        scratch_shapes=[
            pltpu.VMEM((10 * NB, CK, D), BF16),
            pltpu.VMEM((HEADS, 128, BALL), BF16),
            pltpu.VMEM((NB, HEADS, HD, BALL), BF16),
            pltpu.VMEM((NB, HEADS, HD + 8, BALL), F32),
            pltpu.VMEM((LAG, BALL, BALL), BF16),
            pltpu.VMEM((D, BALL), BF16),
            pltpu.VMEM((2 * D, D), BF16),
            pltpu.VMEM((D, D), BF16),
            pltpu.VMEM((256, 256), BF16),
            pltpu.SemaphoreType.DMA((18,)),
            pltpu.SemaphoreType.DMA((18,)),
            pltpu.SemaphoreType.DMA((1,)),
        ],
        compiler_params=pltpu.CompilerParams(
            collective_id=2, has_side_effects=True, vmem_limit_bytes=VMEM_LIMIT),
        name="attention",
    )(chosen, scale, *arrays)


def finish_kernel(slot_ref, pos_ref, res_ref, wg_ref, wu_ref, wd_ref, gain_ref, out_ref,
                  col, ready, landed, send, recv, here):
    greet()

    def back(k):
        return pltpu.make_async_remote_copy(
            src_ref=ready.at[k], dst_ref=landed.at[k], send_sem=send.at[k],
            recv_sem=recv.at[k], device_id={"pts": behind(k)}, device_id_type=MESH)

    own = pltpu.make_async_copy(ready.at[0], landed.at[0], here.at[0])

    def prepare(c, between=None):
        hot = one_hot_cols(0, column(slot_ref[c]), ROWS)
        wide = mm(hot, res_ref[...])
        if between is not None:
            between()
        mean = jnp.mean(wide * wide, axis=-1, keepdims=True)
        ffn = (wide * lax.rsqrt(mean + 1e-5) * gain_ref[...]).astype(BF16)
        gate = mm(ffn, wg_ref[...])
        up = mm(ffn, wu_ref[...])
        hidden = (gate / (1.0 + jnp.exp(-gate)) * up).astype(BF16)
        result = (wide + mm(hidden, wd_ref[...])).astype(BF16)
        ready[pl.ds(pl.multiple_of(c * 8, 8), 8)] = result.reshape(8, EACH, D)

    prepare(0)
    met()

    def more(c):
        first = c * 8 - 8
        prepare(c, lambda: steps(
            jnp.maximum(first, 1), first + 8, lambda k: back(k).start()))

    steps(1, NB, more)
    own.start()
    steps(PEERS - 8, PEERS, lambda k: back(k).start())
    col[...] = column(pos_ref[...])
    own.wait()

    def place(c, store):
        chunk = landed[pl.ds(pl.multiple_of(c * 8, 8), 8)].reshape(256, D)
        for b in range(NB):
            at = slice(b * 256, (b + 1) * 256)
            store(at, mm(one_hot_cols(c * 256, col[at, :], 256), chunk).astype(BF16))

    def arrive(lo, hi):
        steps(lo, hi, lambda k: back(k).wait_recv())

    def set_out(at, part):
        out_ref[at, :] = part

    def add(at, part):
        out_ref[at, :] = out_ref[at, :] + part

    def middle(c):
        arrive(c * 8, c * 8 + 8)
        place(c, add)

    arrive(1, 8)
    place(0, set_out)
    steps(1, NB, middle)
    steps(1, PEERS, lambda k: back(k).wait_send())


def finish(*arrays):
    return pl.pallas_call(
        finish_kernel,
        in_specs=vmem(len(arrays)),
        out_specs=vmem(1)[0],
        out_shape=jax.ShapeDtypeStruct((ROWS, D), BF16),
        scratch_shapes=[
            pltpu.VMEM((ROWS, 1), jnp.int32),
            pltpu.VMEM((PEERS, EACH, D), BF16),
            pltpu.VMEM((PEERS, EACH, D), BF16),
            pltpu.SemaphoreType.DMA((PEERS,)),
            pltpu.SemaphoreType.DMA((PEERS,)),
            pltpu.SemaphoreType.DMA((1,)),
        ],
        compiler_params=pltpu.CompilerParams(
            collective_id=1, has_side_effects=True, vmem_limit_bytes=VMEM_LIMIT),
        name="finish",
    )(*arrays)


def on_device(
    points, point_row_index, neighbour_ball_list, attention_norm_gain, query_weight,
    key_weight, value_weight, pooled_key_weight, pooled_value_weight, head_score_scale,
    output_weight, feedforward_norm_gain, gate_weight, up_weight, down_weight,
):
    me = lax.axis_index("pts")
    grouped, normed, pooled, pos, slot = front(
        point_row_index.reshape(1, ROWS), points, attention_norm_gain.reshape(1, D))
    owner = neighbour_ball_list // NB
    place_of = jnp.mod(owner // 2 - me // 2 + 2, CHIPS) * 2 + owner % 2
    chosen = place_of * NB + neighbour_ball_list % NB
    residual = attention(
        chosen, head_score_scale,
        (normed, grouped, pooled, query_weight, key_weight, value_weight, pooled_key_weight,
         pooled_value_weight, output_weight))
    return finish(slot, pos, residual, gate_weight, up_weight, down_weight,
                  feedforward_norm_gain.reshape(1, D))


def solution(mesh):
    return jax.shard_map(
        on_device,
        mesh=mesh,
        in_specs=(
            P(("rep", "pts"), None), P(("rep", "pts")), P(("rep", "pts"), None),
            P(), P(), P(), P(), P(), P(), P(), P(), P(), P(), P(), P(),
        ),
        out_specs=P(("rep", "pts"), None),
        check_vma=False,
    )
```

```python
import functools
import math

import jax
import jax.numpy as jnp
from jax import lax
from jax.experimental import pallas as pl
from jax.experimental.pallas import tpu as pltpu
from jax.sharding import PartitionSpec as P

BALL = 256
POOL = 8
OWNERS = 4
D = 512
HEADS = 16
HD = 32
FF = 1024
ROWS = 2048
PEERS = 64
EACH = 32
CK = BALL // POOL
NB = ROWS // BALL
STRIDE = 37
LAG = 16
INVERSE = 45
CHIPS = PEERS // 2
MESH = pl.DeviceIdType.MESH
F32 = jnp.float32
BF16 = jnp.bfloat16
VMEM_LIMIT = 56 * 1024 * 1024


def vmem(n):
    return [pl.BlockSpec(memory_space=pltpu.VMEM)] * n


def mm(a, b):
    return jnp.dot(a, b, preferred_element_type=F32)


def mm_nt(a, b):
    return lax.dot_general(a, b, (((1,), (1,)), ((), ())), preferred_element_type=F32)


def one_hot_rows(start, count, row):
    ids = lax.broadcasted_iota(jnp.int32, (count, row.shape[1]), 0) + start
    return jnp.where(ids == row, 1.0, 0.0).astype(BF16)


def one_hot_cols(start, col, width):
    ids = lax.broadcasted_iota(jnp.int32, (col.shape[0], width), 1) + start
    return jnp.where(ids == col, 1.0, 0.0).astype(BF16)


def column(row):
    wide = jnp.broadcast_to(row.astype(F32), (8, row.shape[1]))
    return wide.T[:, :1].astype(jnp.int32)


def ahead(k):
    return (lax.axis_index("pts") + STRIDE * k) % PEERS


def behind(k):
    return (lax.axis_index("pts") + PEERS * STRIDE - STRIDE * k) % PEERS


def greet():
    barrier = pltpu.get_barrier_semaphore()

    def signal(k, carry):
        pl.semaphore_signal(barrier, inc=1, device_id={"pts": ahead(k)}, device_id_type=MESH)
        return carry

    lax.fori_loop(1, PEERS, signal, 0)


def met():
    pl.semaphore_wait(pltpu.get_barrier_semaphore(), PEERS - 1)


def steps(lo, hi, body):
    def step(k, carry):
        body(k)
        return carry

    lax.fori_loop(lo, hi, step, 0)


def front_kernel(
    row_ref, x_ref, gain_ref, grouped_ref, normed_ref, pooled_ref, pos_ref, slot_ref,
    col, ready, numbers, landed, landed_numbers, send, recv, nsend, nrecv, here,
):
    me = lax.axis_index("pts")
    greet()
    row = row_ref[...]
    col[...] = column(row)

    def count(j, acc):
        part = col[pl.ds(pl.multiple_of(j * 256, 256), 256), :]
        less = jnp.where(part < row, 1.0, 0.0)
        return acc + jnp.sum(less.reshape(32, 8, ROWS), axis=0)

    acc = lax.fori_loop(0, NB, count, jnp.zeros((8, ROWS), F32))
    rank = jnp.sum(acc, axis=0, keepdims=True).astype(jnp.int32)
    turn = (((rank >> 5) + PEERS - me) * INVERSE) & (PEERS - 1)
    pos_ref[...] = turn * EACH + (rank & (EACH - 1))
    slot = row & (ROWS - 1)
    parts = jnp.concatenate(
        [(slot >> 6).astype(F32), (slot & 63).astype(F32), jnp.zeros((6, ROWS), F32)],
        axis=0).astype(BF16)

    def rows(k):
        return pltpu.make_async_remote_copy(
            src_ref=ready.at[k], dst_ref=landed.at[k], send_sem=send.at[k],
            recv_sem=recv.at[k], device_id={"pts": ahead(k)}, device_id_type=MESH)

    def ids(k):
        return pltpu.make_async_remote_copy(
            src_ref=numbers.at[k // 4], dst_ref=landed_numbers.at[k], send_sem=nsend.at[k],
            recv_sem=nrecv.at[k], device_id={"pts": ahead(k)}, device_id_type=MESH)

    def start(k):
        ids(k).start()
        rows(k).start()

    def prepare(c, between=None):
        hot = one_hot_rows(c * 256, 256, pos_ref[...])
        if between is not None:
            between()
        ready[pl.ds(pl.multiple_of(c * 8, 8), 8)] = mm(hot, x_ref[...]).astype(BF16).reshape(
            8, EACH, D)
        back = mm_nt(parts, hot)
        whole = (back[0:1] * 64.0 + back[1:2]).astype(jnp.int32)
        numbers[2 * c] = whole[:, :128]
        numbers[2 * c + 1] = whole[:, 128:]

    prepare(0)
    met()
    own = pltpu.make_async_copy(ready.at[0], landed.at[0], here.at[0])
    own_ids = pltpu.make_async_copy(numbers.at[0], landed_numbers.at[0], here.at[1])

    def more(c):
        first = c * 8 - 8
        prepare(c, lambda: steps(jnp.maximum(first, 1), first + 8, start))

    steps(1, NB, more)
    own.start()
    own_ids.start()
    steps(PEERS - 8, PEERS, start)
    own.wait()
    own_ids.wait()

    def place(c, first):
        def arrive(k):
            ids(k).wait_recv()
            rows(k).wait_recv()

        steps(1 if first else c * 8, c * 8 + 8, arrive)
        got = landed_numbers[pl.ds(pl.multiple_of(c * 8, 8), 8)]
        lane = lax.broadcasted_iota(jnp.int32, got.shape, 2) // EACH
        turn = lax.broadcasted_iota(jnp.int32, got.shape, 0) & 3
        got = jnp.where(lane == turn, got, 0)
        halves = [got[0] + got[1] + got[2] + got[3], got[4] + got[5] + got[6] + got[7]]
        number = jnp.concatenate(halves, axis=1)
        slot_ref[c] = number
        chunk = landed[pl.ds(pl.multiple_of(c * 8, 8), 8)].reshape(256, D)
        for b in range(NB):
            at = slice(b * BALL, (b + 1) * BALL)
            part = mm(one_hot_rows(b * BALL, BALL, number), chunk).astype(BF16)
            if first:
                grouped_ref[at, :] = part
            else:
                grouped_ref[at, :] = grouped_ref[at, :] + part

    place(0, True)
    steps(1, NB, lambda c: place(c, False))

    r = lax.broadcasted_iota(jnp.int32, (CK, BALL), 0)
    c = lax.broadcasted_iota(jnp.int32, (CK, BALL), 1)
    pool = jnp.where(c // POOL == r, 1.0 / POOL, 0.0).astype(BF16)

    def norm(b):
        at = pl.ds(pl.multiple_of(b * BALL, BALL), BALL)
        wide = grouped_ref[at, :].astype(F32)
        mean = jnp.mean(wide * wide, axis=-1, keepdims=True)
        normed = (wide * lax.rsqrt(mean + 1e-5) * gain_ref[...]).astype(BF16)
        normed_ref[at, :] = normed
        pooled_ref[b] = mm(pool, normed).astype(BF16)

    steps(0, NB, norm)

    def sent(k):
        ids(k).wait_send()
        rows(k).wait_send()

    steps(1, PEERS, sent)


def front(row, x, gain):
    return pl.pallas_call(
        front_kernel,
        in_specs=vmem(3),
        out_specs=vmem(5),
        out_shape=[
            jax.ShapeDtypeStruct((ROWS, D), BF16),
            jax.ShapeDtypeStruct((ROWS, D), BF16),
            jax.ShapeDtypeStruct((NB, CK, D), BF16),
            jax.ShapeDtypeStruct((1, ROWS), jnp.int32),
            jax.ShapeDtypeStruct((NB, 1, 256), jnp.int32),
        ],
        scratch_shapes=[
            pltpu.VMEM((ROWS, 1), jnp.int32),
            pltpu.VMEM((PEERS, EACH, D), BF16),
            pltpu.VMEM((16, 1, 128), jnp.int32),
            pltpu.VMEM((PEERS, EACH, D), BF16),
            pltpu.VMEM((PEERS, 1, 128), jnp.int32),
            pltpu.SemaphoreType.DMA((PEERS,)),
            pltpu.SemaphoreType.DMA((PEERS,)),
            pltpu.SemaphoreType.DMA((PEERS,)),
            pltpu.SemaphoreType.DMA((PEERS,)),
            pltpu.SemaphoreType.DMA((2,)),
        ],
        compiler_params=pltpu.CompilerParams(
            collective_id=0, has_side_effects=True, vmem_limit_bytes=VMEM_LIMIT),
        name="front",
    )(row, x, gain)


def head_norm_rows(u, mix):
    square = (u * u).astype(BF16)
    mean = jnp.concatenate([mm(square[:, :256], mix), mm(square[:, 256:], mix)], axis=1)
    return (u * lax.rsqrt(mean + 1e-6)).astype(BF16)


def block_ones(rows, per_row, per_col, value):
    a = lax.broadcasted_iota(jnp.int32, (rows, 256), 0) // per_row
    b = lax.broadcasted_iota(jnp.int32, (rows, 256), 1) // per_col
    return jnp.where(a == b, value, 0.0).astype(BF16)


def set_queries(spread, query):
    for h in range(HEADS):
        at = (h % 4) * HD
        spread[h, at:at + HD, :] = query[h]


def head_sums(key, value, spread, probs, finish_head):
    ones = jnp.ones((16, value.shape[1]), BF16)
    count = value.shape[1]

    def scores(h):
        group = slice((h // 4) * 128, (h // 4) * 128 + 128)
        probs[h % LAG, :count, :] = jnp.exp2(mm(key[:, group], spread[h])).astype(BF16)

    def weigh(h):
        rows = jnp.concatenate([value[h * HD:(h + 1) * HD, :], ones], axis=0)
        finish_head(h, mm(rows, probs[h % LAG, :count, :])[:HD + 8])

    for h in range(HEADS + LAG - 1):
        if h < HEADS:
            scores(h)
        if h >= LAG - 1:
            weigh(h - LAG + 1)


def attention_kernel(
    chosen_ref, scale_ref, normed_ref, grouped_ref, pooled_ref, wq_ref, wk_ref, wv_ref,
    wpk_ref, wpv_ref, wo_ref, out_ref,
    cand, spread, queries, totals, probs, turned, wqv_t, wpv_t, mix, send, recv, here,
):
    me = lax.axis_index("pts")
    core = me % 2
    chip = me // 2
    partner = chip * 2 + 1 - core
    def chip_at(e):
        return ((chip + e + CHIPS) % CHIPS) * 2 + core

    barrier = pltpu.get_barrier_semaphore()
    for d in (partner, chip_at(1), chip_at(-1)):
        pl.semaphore_signal(barrier, inc=1, device_id={"pts": d}, device_id_type=MESH)
    pl.semaphore_wait(barrier, 3)

    half = NB // 2

    def slot(e):
        return (2 - e) * 2 + core

    def part(at, h):
        return cand.at[pl.ds(at * NB + h * half, half)]

    def remote(src, at, h, sem, d):
        return pltpu.make_async_remote_copy(
            src_ref=src, dst_ref=part(at, h), send_sem=send.at[sem], recv_sem=recv.at[sem],
            device_id={"pts": d}, device_id_type=MESH)

    def mine(h):
        return pooled_ref.at[pl.ds(h * half, half)]

    sides = (1, -1)
    outs = [[remote(mine(h), slot(e), h, h * 2 + i, chip_at(e)) for i, e in enumerate(sides)]
            for h in range(2)]
    farther = [[remote(part(slot(e), h), slot(2 * e), h, 4 + h * 2 + i, chip_at(e))
                for i, e in enumerate(sides)] for h in range(2)]
    onward = [[remote(part(slot(e), h), slot(e), h, 8 + h * 4 + i, partner)
               for i, e in enumerate((1, -1, 2, -2))] for h in range(2)]
    to_partner = [remote(mine(h), slot(0), h, 16 + h, partner) for h in range(2)]
    for copy in outs[0] + outs[1] + to_partner:
        copy.start()
    own = pltpu.make_async_copy(pooled_ref, cand.at[pl.ds(slot(0) * NB, NB)], here.at[0])
    own.start()

    spread[...] = jnp.zeros_like(spread)
    wqv_t[:D, :] = wq_ref[...].T
    wqv_t[D:, :] = wv_ref[...].T
    wpv_t[...] = wpv_ref[...].T
    mix[...] = block_ones(256, HD, HD, 1.0 / HD)

    def near(ball, carry):
        for h, at in enumerate((3, 4)):
            @pl.when(ball == at)
            def _():
                for i in range(2):
                    outs[h][i].wait_recv()
                    farther[h][i].start()
                    onward[h][i].start()

        for h, at in enumerate((6, 7)):
            @pl.when(ball == at)
            def _():
                for i in range(2):
                    farther[h][i].wait_recv()
                    onward[h][2 + i].start()

        rows = pl.ds(pl.multiple_of(ball * BALL, BALL), BALL)
        normed = normed_ref[rows, :]
        both = mm_nt(wqv_t[...], normed)
        shaped = both[:D].reshape(HEADS, HD, BALL)
        mean = jnp.mean(shaped * shaped, axis=1, keepdims=True)
        factor = lax.rsqrt(mean + 1e-6)
        for h in range(HEADS):
            queries[ball, h] = (shaped[h] * (factor[h] * (scale_ref[h] * (math.log2(math.e) / HD)))).astype(BF16)
        value = both[D:].astype(BF16)
        key = head_norm_rows(mm(normed, wk_ref[...]), mix[...])
        set_queries(spread, queries.at[ball])

        def keep(h, total):
            totals[ball, h] = total

        head_sums(key, value, spread, probs, keep)
        return carry

    lax.fori_loop(0, NB, near, 0)
    own.wait()
    for h in range(2):
        to_partner[h].wait()
        for copy in outs[h] + farther[h]:
            copy.wait_send()
        for copy in onward[h]:
            copy.wait()

    def far(ball, carry):
        rows = pl.ds(pl.multiple_of(ball * BALL, BALL), BALL)
        picked = []
        for j in range(OWNERS):
            picked.append(cand[chosen_ref[ball, j]])
        picked = jnp.concatenate(picked, axis=0)
        key = head_norm_rows(mm(picked, wpk_ref[...]), mix[...])
        value = mm_nt(wpv_t[...], picked).astype(BF16)
        set_queries(spread, queries.at[ball])

        def close(h, total):
            total = totals[ball, h] + total
            turned[h * HD:(h + 1) * HD, :] = (total[:HD] / total[HD:HD + 1]).astype(BF16)

        head_sums(key, value, spread, probs, close)
        attended = turned[...].T
        out_ref[rows, :] = (
            grouped_ref[rows, :].astype(F32) + mm(attended, wo_ref[...])).astype(BF16)
        return carry

    lax.fori_loop(0, NB, far, 0)


def attention(chosen, scale, arrays):
    return pl.pallas_call(
        attention_kernel,
        in_specs=[pl.BlockSpec(memory_space=pltpu.SMEM)] * 2 + vmem(len(arrays)),
        out_specs=vmem(1)[0],
        out_shape=jax.ShapeDtypeStruct((ROWS, D), BF16),
        scratch_shapes=[
            pltpu.VMEM((10 * NB, CK, D), BF16),
            pltpu.VMEM((HEADS, 128, BALL), BF16),
            pltpu.VMEM((NB, HEADS, HD, BALL), BF16),
            pltpu.VMEM((NB, HEADS, HD + 8, BALL), F32),
            pltpu.VMEM((LAG, BALL, BALL), BF16),
            pltpu.VMEM((D, BALL), BF16),
            pltpu.VMEM((2 * D, D), BF16),
            pltpu.VMEM((D, D), BF16),
            pltpu.VMEM((256, 256), BF16),
            pltpu.SemaphoreType.DMA((18,)),
            pltpu.SemaphoreType.DMA((18,)),
            pltpu.SemaphoreType.DMA((1,)),
        ],
        compiler_params=pltpu.CompilerParams(
            collective_id=2, has_side_effects=True, vmem_limit_bytes=VMEM_LIMIT),
        name="attention",
    )(chosen, scale, *arrays)


def finish_kernel(slot_ref, pos_ref, res_ref, wg_ref, wu_ref, wd_ref, gain_ref, out_ref,
                  col, ready, landed, send, recv, here):
    greet()

    def back(k):
        return pltpu.make_async_remote_copy(
            src_ref=ready.at[k], dst_ref=landed.at[k], send_sem=send.at[k],
            recv_sem=recv.at[k], device_id={"pts": behind(k)}, device_id_type=MESH)

    own = pltpu.make_async_copy(ready.at[0], landed.at[0], here.at[0])

    def prepare(c, between=None):
        hot = one_hot_cols(0, column(slot_ref[c]), ROWS)
        wide = mm(hot, res_ref[...])
        if between is not None:
            between()
        mean = jnp.mean(wide * wide, axis=-1, keepdims=True)
        ffn = (wide * lax.rsqrt(mean + 1e-5) * gain_ref[...]).astype(BF16)
        gate = mm(ffn, wg_ref[...])
        up = mm(ffn, wu_ref[...])
        hidden = (gate / (1.0 + jnp.exp(-gate)) * up).astype(BF16)
        result = (wide + mm(hidden, wd_ref[...])).astype(BF16)
        ready[pl.ds(pl.multiple_of(c * 8, 8), 8)] = result.reshape(8, EACH, D)

    prepare(0)
    met()

    def more(c):
        first = c * 8 - 8
        prepare(c, lambda: steps(
            jnp.maximum(first, 1), first + 8, lambda k: back(k).start()))

    steps(1, NB, more)
    own.start()
    steps(PEERS - 8, PEERS, lambda k: back(k).start())
    col[...] = column(pos_ref[...])
    own.wait()

    def place(c, store):
        chunk = landed[pl.ds(pl.multiple_of(c * 8, 8), 8)].reshape(256, D)
        for b in range(NB):
            at = slice(b * 256, (b + 1) * 256)
            store(at, mm(one_hot_cols(c * 256, col[at, :], 256), chunk).astype(BF16))

    def arrive(lo, hi):
        steps(lo, hi, lambda k: back(k).wait_recv())

    def set_out(at, part):
        out_ref[at, :] = part

    def add(at, part):
        out_ref[at, :] = out_ref[at, :] + part

    def middle(c):
        arrive(c * 8, c * 8 + 8)
        place(c, add)

    arrive(1, 8)
    place(0, set_out)
    steps(1, NB, middle)
    steps(1, PEERS, lambda k: back(k).wait_send())


def finish(*arrays):
    return pl.pallas_call(
        finish_kernel,
        in_specs=vmem(len(arrays)),
        out_specs=vmem(1)[0],
        out_shape=jax.ShapeDtypeStruct((ROWS, D), BF16),
        scratch_shapes=[
            pltpu.VMEM((ROWS, 1), jnp.int32),
            pltpu.VMEM((PEERS, EACH, D), BF16),
            pltpu.VMEM((PEERS, EACH, D), BF16),
            pltpu.SemaphoreType.DMA((PEERS,)),
            pltpu.SemaphoreType.DMA((PEERS,)),
            pltpu.SemaphoreType.DMA((1,)),
        ],
        compiler_params=pltpu.CompilerParams(
            collective_id=1, has_side_effects=True, vmem_limit_bytes=VMEM_LIMIT),
        name="finish",
    )(*arrays)


def on_device(
    points, point_row_index, neighbour_ball_list, attention_norm_gain, query_weight,
    key_weight, value_weight, pooled_key_weight, pooled_value_weight, head_score_scale,
    output_weight, feedforward_norm_gain, gate_weight, up_weight, down_weight,
):
    me = lax.axis_index("pts")
    grouped, normed, pooled, pos, slot = front(
        point_row_index.reshape(1, ROWS), points, attention_norm_gain.reshape(1, D))
    owner = neighbour_ball_list // NB
    place_of = jnp.mod(owner // 2 - me // 2 + 2, CHIPS) * 2 + owner % 2
    chosen = place_of * NB + neighbour_ball_list % NB
    residual = attention(
        chosen, head_score_scale,
        (normed, grouped, pooled, query_weight, key_weight, value_weight, pooled_key_weight,
         pooled_value_weight, output_weight))
    return finish(slot, pos, residual, gate_weight, up_weight, down_weight,
                  feedforward_norm_gain.reshape(1, D))


def solution(mesh):
    return jax.shard_map(
        on_device,
        mesh=mesh,
        in_specs=(
            P(("rep", "pts"), None), P(("rep", "pts")), P(("rep", "pts"), None),
            P(), P(), P(), P(), P(), P(), P(), P(), P(), P(), P(), P(),
        ),
        out_specs=P(("rep", "pts"), None),
        check_vma=False,
    )
```
